32 devices in a mesh: dp: 16 (over z, y, core), rep: 2 (over x).
Axes of the slice: x: 2, y: 2, z: 4, core: 2. Of those that a mesh axis runs over, the one named last changes fastest.
Arguments:
- tokens: bfloat16 [512, 2048], P(('dp', 'rep')), may hold values from -6 to 6
- norm_gain: float32 [2048], replicated, may hold values from 0.1 to 1.9
- expert_weights: bfloat16 [8, 2048, 2304], P(None, ('dp', 'rep')), may hold values from -0.125 to 0.125
- slot_expert: int32 [16], replicated, may hold values from 0 to 7, as said below
- pair_slots: int32 [512, 8], P(('dp', 'rep')), may hold values from 0 to 15, all different within a row; in each aligned block of 16 rows (0 to 15, 16 to 31, ...) at most 16 rows name the same one
- combine_weights: float32 [512, 8], P(('dp', 'rep')), may hold values from 0.25 to 2
Outputs:
- layer_out: bfloat16 [512, 2048], P(('dp', 'rep'))
The draws below stay inside these ranges and needn't reach their ends.
Inputs may be any that keep to these rules, and one draw needn't show every extreme that they name: `slot_expert`: every one of the 8 experts is held by at least one slot. `pair_slots`: each row names 8 different slots; among the 16 rows of one device no slot is named by more than 16 rows.
All inputs are finite; a program needn't handle non-finite values.
Results may differ from the reference program's by a relative error of at most 0.0071.
Values may be sent and summed in bfloat16 or wider, within the bound.
No kernel may reach another device: no remote copies, remote signals or barrier semaphores. Data moves between devices by JAX's collectives and lax.ppermute only.
A program may use at most 64 MiB of HBM per device.

```python
import math
import jax
import jax.numpy as jnp
import numpy as np
from jax import lax

D = 2048
F = 768
TOPK = 8
TOK_DEV = 16
SLOTS = 16
EXPERTS = 8
CAP = 16
TOKENS = 512
N_DP = 16


def draw_slot_expert(key, part):
    first_key = jax.random.fold_in(key, 11)
    second_key = jax.random.fold_in(key, 23)
    third_key = jax.random.fold_in(key, 37)
    hot_count = max(1, EXPERTS // 4)
    favoured = jax.random.permutation(first_key, EXPERTS)[:hot_count].astype(jnp.int32)
    extras = favoured[jax.random.randint(second_key, (SLOTS - EXPERTS,), 0, hot_count)]
    listing = jnp.concatenate([jnp.arange(EXPERTS, dtype=jnp.int32), extras.astype(jnp.int32)])
    return listing[jax.random.permutation(third_key, SLOTS)].astype(jnp.int32)


def block_scale(rng, extent, pieces, least, high):
    level = 1.0
    for axis_at, blocks in pieces:
        draws = jax.random.uniform(jax.random.fold_in(jax.random.fold_in(rng, 6), axis_at), (blocks,), jnp.float32, least / len(pieces), high / len(pieces))
        level = level * jnp.repeat(jnp.exp(draws), extent[axis_at] // blocks).reshape((-1,) + (1,) * (len(extent) - 1 - axis_at))
    return level


def assign_block(key, own, number, rows, count, top, bound, skew):
    order = jax.random.permutation(key, count)
    heavy_load, usual = portions_of(count, rows * top, bound, skew, True), portions_of(count, rows * top, bound, skew, False)
    places = jnp.arange(count)

    def named(sizes, rotation):
        used = int((sizes > 0).sum())
        fixed = max(1, used // 4)
        shifted = fixed + (places - fixed + rotation * (used - fixed)) % max(1, count - fixed)
        return jnp.zeros((count,), jnp.int32).at[order[jnp.where(places < fixed, places, shifted)]].set(jnp.asarray(sizes, jnp.int32))

    sizes = jnp.where(number % 4 == 0, named(heavy_load, number // 4), named(usual, number - number // 4 - 1))
    mixed = jax.random.permutation(jax.random.fold_in(own, 3), count)
    donor, receiver = mixed[0:count // 2 * 2:2], mixed[1:count // 2 * 2:2]
    room = jnp.minimum(sizes[donor] - 1, bound - sizes[receiver]) // 2
    room = jnp.where((donor == order[0]) | (receiver == order[0]) | (sizes[receiver] == 0), 0, jnp.maximum(room, 0))
    shifted = jax.random.randint(jax.random.fold_in(own, 4), (count // 2,), 0, 1 << 20) % (room + 1)
    sizes = sizes.at[donor].add(-shifted).at[receiver].add(shifted)
    labels = jnp.searchsorted(jnp.cumsum(sizes), jnp.arange(rows * top), side="right").astype(jnp.int32)
    table = labels.reshape(top, rows).T
    table = table[jax.random.permutation(jax.random.fold_in(own, 1), rows)]
    rotation = jax.random.randint(jax.random.fold_in(own, 2), (rows, 1), 0, top)
    return jnp.take_along_axis(table, (jnp.arange(top)[None, :] + rotation) % top, axis=1)


def portions_of(amount, total, limit, slope, full):
    portions = [(1 << 20) // math.isqrt(grade ** slope) + 1 for grade in range(1, amount + 1)]
    largest = limit if full else min(limit, max(-(-total // amount), total * portions[0] // sum(portions)))
    least = 1 if total - largest >= amount - 1 else 0
    given, surplus = [largest] + [least] * (amount - 1), total - largest - least * (amount - 1)
    while surplus > 0:
        free = [i for i in range(1, amount) if given[i] < largest] or [i for i in range(1, amount) if given[i] < limit]
        pool, budget = sum([portions[i] for i in free]), surplus
        for i in free:
            more = min(limit - given[i], max(1, budget * portions[i] // pool), surplus)
            given[i] = given[i] + more
            surplus = surplus - more
    return np.array(given)


def noise(stream_key, dims, spread, bound, pieces=(), kind=jnp.bfloat16):
    gain = block_scale(stream_key, dims, pieces, -0.22, 0.18) if pieces else 1.0
    array = jax.random.normal(stream_key, dims, jnp.float32) * spread * gain
    return jnp.minimum(jnp.maximum(array, -bound), bound).astype(kind)


def setup_inputs(seed: int = 0) -> dict:
    arg_keys = jax.random.split(jax.random.key(seed), 7)
    tokens = noise(arg_keys[0], (TOKENS, D), 1.0, 6.0, ((0, 32),))
    norm_gain = jnp.clip(1.0 + 0.18 * jax.random.normal(arg_keys[1], (D,), jnp.float32), 0.1, 1.9)
    expert_weights = noise(arg_keys[2], (EXPERTS, D, 3 * F), D ** -0.5, 0.125, ((1, 32),))
    slot_expert = draw_slot_expert(jax.random.fold_in(arg_keys[6], 71), 0)
    pair_slots_keys = jax.random.split(jax.random.fold_in(arg_keys[4], 1), TOKENS // TOK_DEV)
    pair_slots_turns = jax.random.permutation(jax.random.fold_in(arg_keys[4], 3), TOKENS // TOK_DEV)
    pair_slots = jax.vmap(lambda own, number: assign_block(jax.random.fold_in(arg_keys[4], 2), own, number, TOK_DEV, SLOTS, TOPK, CAP, 2))(pair_slots_keys, pair_slots_turns).reshape((TOKENS, TOPK))
    combine_weights = jnp.clip(jnp.exp(math.log(2.0) - 2.0794415 * jax.random.uniform(arg_keys[5], (TOKENS, TOPK), jnp.float32) ** block_scale(arg_keys[5], (TOKENS, TOPK), ((0, 32),), -0.2, 0.2)), 0.25, 2.0)
    return {"tokens": tokens, "norm_gain": norm_gain, "expert_weights": expert_weights, "slot_expert": slot_expert, "pair_slots": pair_slots, "combine_weights": combine_weights}


def reference(tokens, norm_gain, expert_weights, slot_expert, pair_slots, combine_weights):
    values = tokens.astype(jnp.float32)
    mean_square = lax.optimization_barrier(jnp.mean(values * values, axis=1, keepdims=True))
    normed = (values * lax.rsqrt(mean_square + 1e-06) * norm_gain[None, :]).astype(jnp.bfloat16)
    device_count = TOKENS // TOK_DEV
    pair_count = TOK_DEV * TOPK
    targets = pair_slots.reshape(device_count, pair_count).astype(jnp.int32)
    onehot = (targets[:, :, None] == jnp.arange(N_DP, dtype=jnp.int32)[None, None, :]).astype(jnp.int32)
    before = jnp.cumsum(onehot, axis=1) - onehot
    position = lax.optimization_barrier(jnp.sum(before * onehot, axis=2)).astype(jnp.int32)
    column = (jnp.arange(device_count, dtype=jnp.int32)[:, None] * CAP + position).astype(jnp.int32)
    pair_index = jnp.arange(device_count * pair_count, dtype=jnp.int32).reshape(device_count, pair_count)
    inverse = jnp.full((N_DP, device_count * CAP), -1, jnp.int32).at[targets, column].set(pair_index)

    def per_slot(inputs):
        slot_pairs, expert = inputs
        valid = slot_pairs >= 0
        token_rows = jnp.maximum(slot_pairs, 0) // TOPK
        rows = jnp.where(valid[:, None], normed[token_rows], jnp.zeros((), jnp.bfloat16))
        weight = expert_weights[expert]
        gate_up = jnp.dot(rows, weight[:, :2 * F], preferred_element_type=jnp.float32)
        hidden = (jax.nn.silu(gate_up[:, :F]) * gate_up[:, F:]).astype(jnp.bfloat16)
        return jnp.dot(hidden, weight[:, 2 * F:].T, preferred_element_type=jnp.float32).astype(jnp.bfloat16)
    outputs = lax.map(per_slot, (inverse, slot_expert.astype(jnp.int32)))
    expert_out = outputs[targets, column].astype(jnp.float32).reshape(TOKENS, TOPK, D)
    mixed = lax.optimization_barrier(jnp.sum(expert_out * combine_weights[:, :, None], axis=1))
    return mixed.astype(jnp.bfloat16)
```

```python
import functools
import jax
import jax.numpy as jnp
from jax import lax
from jax.sharding import Mesh, PartitionSpec as P

SWAP = [(0, 1), (1, 0)]


def normalize(tokens, norm_gain):
    values = tokens.astype(jnp.float32)
    mean_square = jnp.mean(values * values, axis=1, keepdims=True)
    return (values * lax.rsqrt(mean_square + 1e-06) * norm_gain[None, :]).astype(jnp.bfloat16)


def dense_layer(tokens, norm_gain, expert_weights, slot_expert, pair_slots, combine_weights):
    experts, own_rows, packed = expert_weights.shape
    token_count, width = tokens.shape
    hidden_units = packed // 3
    part = hidden_units // 2
    half_axes = ("z", "y", "c", "x")
    chip_axes = ("z", "y", "x")
    everywhere = ("h",) + half_axes
    nz, ny, nx = (lax.axis_size(a) for a in chip_axes)
    chips = nz * ny * nx
    peers = 2 * chips
    blocks = expert_weights.reshape(nz, ny, nx, own_rows, 3, 2, part)
    blocks = blocks.transpose(0, 1, 5, 2, 3, 4, 6)
    gate_up = blocks[:, :, :, :, :, :2].reshape(peers, own_rows, 2 * part)
    down = blocks[:, :, :, :, :, 2].reshape(1, peers, own_rows, part)
    down = jnp.broadcast_to(down, (2, peers, own_rows, part)).reshape(2 * peers, own_rows, part)
    gate_up = lax.all_to_all(gate_up, half_axes, 0, 0, tiled=True).reshape(peers * own_rows, 2 * part)
    normed = normalize(tokens, norm_gain)
    h = lax.axis_index("h")
    halves = normed.reshape(token_count, 2, width // 2)
    mine = lax.dynamic_index_in_dim(halves, h, 1, keepdims=False)
    other = lax.dynamic_index_in_dim(halves, 1 - h, 1, keepdims=False)
    near = jnp.stack([mine, lax.ppermute(other, "h", SWAP)])
    spread = jnp.broadcast_to(near[None], (chips,) + near.shape)
    spread = lax.all_to_all(spread, chip_axes, 0, 0, tiled=True)
    spread = spread.transpose(1, 0, 2, 3).reshape(2, chips * token_count, width // 2)
    crossed = lax.ppermute(spread, "c", SWAP)
    rows = jnp.concatenate([spread[:, None], crossed[:, None]], axis=1)
    rows = rows.reshape(4 * chips * token_count, width // 2)
    down = lax.all_to_all(down, everywhere, 0, 0, tiled=True).reshape(width, part)
    partial = jnp.dot(rows, gate_up, preferred_element_type=jnp.float32)
    mid = partial.shape[0] // 2
    arrived = lax.ppermute(partial[mid:].astype(jnp.bfloat16), "h", SWAP)
    pre = partial[:mid] + arrived.astype(jnp.float32)
    hidden = (jax.nn.silu(pre[:, :part]) * pre[:, part:]).astype(jnp.bfloat16)
    result = lax.dot_general(hidden, down, (((1,), (1,)), ((), ())), preferred_element_type=jnp.float32)
    quarter = mid // 2
    arrived = lax.ppermute(result[quarter:].astype(jnp.bfloat16), "c", SWAP)
    result = (result[:quarter] + arrived.astype(jnp.float32)).astype(jnp.bfloat16)
    result = result.reshape(chips, token_count, width)
    returned = lax.all_to_all(result, chip_axes, 0, 0, tiled=True).astype(jnp.float32)
    chosen = jnp.sum(
        jnp.where(
            pair_slots[:, :, None] == jnp.arange(slot_expert.shape[0], dtype=jnp.int32)[None, None, :],
            slot_expert[None, None, :],
            0,
        ),
        axis=2,
    )
    coefficient = jnp.sum(
        jnp.where(
            chosen[:, :, None] == jnp.arange(experts, dtype=jnp.int32)[None, None, :],
            combine_weights[:, :, None],
            0.0,
        ),
        axis=1,
    )
    mixed = jnp.sum(returned * coefficient.T[:, :, None], axis=0)
    return mixed.astype(jnp.bfloat16)


def per_device(tokens, norm_gain, expert_weights, slot_expert, pair_slots, combine_weights):
    slot_count = lax.axis_size("dp")
    model_width = tokens.shape[1]
    packed_width = expert_weights.shape[2]
    hidden_units = packed_width // 3
    token_count = tokens.shape[0]
    choice_count = pair_slots.shape[1]
    pair_count = token_count * choice_count
    capacity = max(2, 2 * pair_count // slot_count)
    outgoing = jnp.take(expert_weights, slot_expert, axis=0)
    arrived = lax.all_to_all(outgoing, "dp", split_axis=0, concat_axis=0, tiled=True)
    assembled = lax.all_gather(arrived[:, None], "rep", axis=1, tiled=True)
    weight = assembled.reshape(model_width, packed_width)
    values = tokens.astype(jnp.float32)
    mean_square = jnp.mean(values * values, axis=1, keepdims=True)
    normed = (values * lax.rsqrt(mean_square + 1e-06) * norm_gain[None, :]).astype(jnp.bfloat16)
    targets = pair_slots.reshape(pair_count)
    onehot = (targets[:, None] == jnp.arange(slot_count, dtype=jnp.int32)[None, :]).astype(
        jnp.int32
    )
    before = jnp.cumsum(onehot, axis=0) - onehot
    position = jnp.sum(before * onehot, axis=1)
    target_row = targets * capacity + position
    selector = (
        jnp.arange(slot_count * capacity, dtype=jnp.int32)[:, None] == target_row[None, :]
    ).astype(jnp.bfloat16)
    pair_rows = jnp.repeat(normed, choice_count, axis=0)
    outbound = jnp.dot(selector, pair_rows, preferred_element_type=jnp.float32).astype(jnp.bfloat16)
    outbound = outbound.reshape(slot_count, capacity, model_width)
    rows = lax.all_to_all(outbound, "dp", split_axis=0, concat_axis=0, tiled=True).reshape(
        -1, model_width
    )
    gate_up = jnp.dot(rows, weight[:, : 2 * hidden_units], preferred_element_type=jnp.float32)
    hidden = (jax.nn.silu(gate_up[:, :hidden_units]) * gate_up[:, hidden_units:]).astype(
        jnp.bfloat16
    )
    result = lax.dot_general(
        hidden,
        weight[:, 2 * hidden_units :],
        (((1,), (1,)), ((), ())),
        preferred_element_type=jnp.float32,
    )
    result = result.astype(jnp.bfloat16).reshape(slot_count, -1, model_width)
    returned = lax.all_to_all(result, "dp", split_axis=0, concat_axis=0, tiled=True)
    expert_out = jnp.dot(
        selector.T,
        returned.reshape(slot_count * capacity, model_width),
        preferred_element_type=jnp.float32,
    )
    expert_out = expert_out.reshape(token_count, choice_count, model_width)
    mixed = jnp.sum(expert_out * combine_weights[:, :, None], axis=1)
    return mixed.astype(jnp.bfloat16)


def solution(mesh):
    slots, engines = mesh.shape["dp"], mesh.shape["rep"]

    def layer(tokens, norm_gain, expert_weights, slot_expert, pair_slots, combine_weights):
        experts, _, packed = expert_weights.shape
        dense = slots % 8 == 0 and slots * engines == 4 * experts and packed % 6 == 0
        if dense:
            devices = mesh.devices.reshape(2, slots // 8, 2, 2, engines)
            inner, split = Mesh(devices, ("h", "z", "y", "c", "x")), ("h", "z", "y", "c", "x")
        else:
            inner, split = mesh, ("dp", "rep")
        placed = (P(split, None), P(), P(None, split, None), P(), P(split, None), P(split, None))
        return jax.shard_map(
            dense_layer if dense else per_device,
            mesh=inner,
            in_specs=placed,
            out_specs=P(split, None),
            check_vma=False,
        )(tokens, norm_gain, expert_weights, slot_expert, pair_slots, combine_weights)

    return layer
```

```python
import jax
import jax.numpy as jnp
from jax import lax
from jax.sharding import Mesh, PartitionSpec as P

SWAP = [(0, 1), (1, 0)]
CROSS = [(0, 3), (1, 2), (2, 1), (3, 0)]


def normalize(tokens, norm_gain):
    values = tokens.astype(jnp.float32)
    mean_square = jnp.mean(values * values, axis=1, keepdims=True)
    return (values * lax.rsqrt(mean_square + 1e-06) * norm_gain[None, :]).astype(jnp.bfloat16)


def in_order(bit, near, far, axis):
    return jnp.where(
        bit == 0, jnp.concatenate([near, far], axis=axis), jnp.concatenate([far, near], axis=axis)
    )


def slot_coefficients(slot_expert, pair_slots, combine_weights, experts):
    slots = jnp.arange(slot_expert.shape[0], dtype=jnp.int32)
    held = slot_expert[None, None, :]
    chosen = jnp.sum(jnp.where(pair_slots[:, :, None] == slots[None, None, :], held, 0), axis=2)
    numbers = jnp.arange(experts, dtype=jnp.int32)
    weights = combine_weights[:, :, None]
    return jnp.sum(jnp.where(chosen[:, :, None] == numbers[None, None, :], weights, 0.0), axis=1)


def dense_layer(tokens, norm_gain, expert_weights, slot_expert, pair_slots, combine_weights):
    experts, own_rows, packed = expert_weights.shape
    token_count, width = tokens.shape
    hidden_units = packed // 3
    chip_axes = ("z", "y", "x")
    chips = experts
    engines = lax.axis_size("x")
    h, c = lax.axis_index("h"), lax.axis_index("c")
    group = engines * own_rows
    groups = width // (4 * group)

    far_down = lax.ppermute(expert_weights[:, :, 2 * hidden_units :], "h", SWAP)
    weights = lax.all_to_all(expert_weights, chip_axes, 0, 0, tiled=True)
    far_down = lax.all_to_all(far_down, chip_axes, 0, 0, tiled=True)
    gate_up = weights[:, :, : 2 * hidden_units].reshape(chips * own_rows, 2 * hidden_units)
    near_down = weights[:, :, 2 * hidden_units :].reshape(chips * own_rows, hidden_units)
    far_down = far_down.reshape(chips * own_rows, hidden_units)

    normed = normalize(tokens, norm_gain)
    pieces = [
        jnp.concatenate(
            [normed[:, ((i * groups + g) * 2 + j) * group :][:, :group] for g in range(groups)], axis=1
        )
        for i in range(2)
        for j in range(2)
    ]

    def piece(i, j):
        at = 2 * i + j
        return jnp.where(
            at < 2, jnp.where(at == 0, pieces[0], pieces[1]), jnp.where(at == 2, pieces[2], pieces[3])
        )

    rows = jnp.stack(
        [
            piece(h, c),
            lax.ppermute(piece(h, 1 - c), "c", SWAP),
            lax.ppermute(piece(1 - h, c), "h", SWAP),
            lax.ppermute(piece(1 - h, 1 - c), ("h", "c"), CROSS),
        ]
    )
    for axis in ("x", "y", "z"):
        rows = in_order(lax.axis_index(axis), rows, lax.ppermute(rows, axis, SWAP), 1)
    count = chips * token_count

    def products(first):
        block = rows[first : first + 2].reshape(2 * count, -1)
        sums = jnp.dot(block, gate_up, preferred_element_type=jnp.float32)
        arrived = lax.ppermute(sums[count:].astype(jnp.bfloat16), "c", SWAP)
        return sums[:count] + arrived.astype(jnp.float32)

    far = lax.ppermute(products(2).astype(jnp.bfloat16), "h", SWAP)
    pre = products(0) + far.astype(jnp.float32)
    hidden = (jax.nn.silu(pre[:, :hidden_units]) * pre[:, hidden_units:]).astype(jnp.bfloat16)
    hidden = in_order(c, hidden, lax.ppermute(hidden, "c", SWAP), 0)

    def result(down):
        return lax.dot_general(
            hidden, down, (((1,), (1,)), ((), ())), preferred_element_type=jnp.float32
        ).astype(jnp.bfloat16)

    outbound = jnp.concatenate([result(near_down), result(far_down)], axis=1)
    outbound = outbound.reshape(2 * chips, token_count, width // 2)
    returned = lax.all_to_all(outbound, ("c",) + chip_axes, 0, 0, tiled=True)
    returned = returned.reshape(2, chips, token_count, width // 2).astype(jnp.float32)
    coefficient = slot_coefficients(slot_expert, pair_slots, combine_weights, experts)
    mixed = jnp.sum(returned * coefficient.T[None, :, :, None], axis=1).astype(jnp.bfloat16)
    mixed = in_order(h, mixed[:, :, : width // 4], mixed[:, :, width // 4 :], 2)
    spans = [mixed[j, :, g * group : (g + 1) * group] for g in range(2 * groups) for j in range(2)]
    return jnp.concatenate(spans, axis=1)


def per_device(tokens, norm_gain, expert_weights, slot_expert, pair_slots, combine_weights):
    slot_count = lax.axis_size("dp")
    model_width = tokens.shape[1]
    packed_width = expert_weights.shape[2]
    hidden_units = packed_width // 3
    token_count = tokens.shape[0]
    choice_count = pair_slots.shape[1]
    pair_count = token_count * choice_count
    capacity = max(2, 2 * pair_count // slot_count)
    outgoing = jnp.take(expert_weights, slot_expert, axis=0)
    arrived = lax.all_to_all(outgoing, "dp", split_axis=0, concat_axis=0, tiled=True)
    assembled = lax.all_gather(arrived[:, None], "rep", axis=1, tiled=True)
    weight = assembled.reshape(model_width, packed_width)
    values = tokens.astype(jnp.float32)
    mean_square = jnp.mean(values * values, axis=1, keepdims=True)
    normed = (values * lax.rsqrt(mean_square + 1e-06) * norm_gain[None, :]).astype(jnp.bfloat16)
    targets = pair_slots.reshape(pair_count)
    onehot = (targets[:, None] == jnp.arange(slot_count, dtype=jnp.int32)[None, :]).astype(
        jnp.int32
    )
    before = jnp.cumsum(onehot, axis=0) - onehot
    position = jnp.sum(before * onehot, axis=1)
    target_row = targets * capacity + position
    selector = (
        jnp.arange(slot_count * capacity, dtype=jnp.int32)[:, None] == target_row[None, :]
    ).astype(jnp.bfloat16)
    pair_rows = jnp.repeat(normed, choice_count, axis=0)
    outbound = jnp.dot(selector, pair_rows, preferred_element_type=jnp.float32).astype(jnp.bfloat16)
    outbound = outbound.reshape(slot_count, capacity, model_width)
    rows = lax.all_to_all(outbound, "dp", split_axis=0, concat_axis=0, tiled=True).reshape(
        -1, model_width
    )
    gate_up = jnp.dot(rows, weight[:, : 2 * hidden_units], preferred_element_type=jnp.float32)
    hidden = (jax.nn.silu(gate_up[:, :hidden_units]) * gate_up[:, hidden_units:]).astype(
        jnp.bfloat16
    )
    result = lax.dot_general(
        hidden,
        weight[:, 2 * hidden_units :],
        (((1,), (1,)), ((), ())),
        preferred_element_type=jnp.float32,
    )
    result = result.astype(jnp.bfloat16).reshape(slot_count, -1, model_width)
    returned = lax.all_to_all(result, "dp", split_axis=0, concat_axis=0, tiled=True)
    expert_out = jnp.dot(
        selector.T,
        returned.reshape(slot_count * capacity, model_width),
        preferred_element_type=jnp.float32,
    )
    expert_out = expert_out.reshape(token_count, choice_count, model_width)
    mixed = jnp.sum(expert_out * combine_weights[:, :, None], axis=1)
    return mixed.astype(jnp.bfloat16)


def solution(mesh):
    slots, engines = mesh.shape["dp"], mesh.shape["rep"]

    def layer(tokens, norm_gain, expert_weights, slot_expert, pair_slots, combine_weights):
        experts = expert_weights.shape[0]
        dense = engines == 2 and slots == 2 * experts and slots % 8 == 0 and slots <= 16
        if dense:
            devices = mesh.devices.reshape(2, slots // 8, 2, 2, engines)
            inner, split = Mesh(devices, ("h", "z", "y", "c", "x")), ("h", "z", "y", "c", "x")
        else:
            inner, split = mesh, ("dp", "rep")
        placed = (P(split, None), P(), P(None, split, None), P(), P(split, None), P(split, None))
        return jax.shard_map(
            dense_layer if dense else per_device,
            mesh=inner,
            in_specs=placed,
            out_specs=P(split, None),
            check_vma=False,
        )(tokens, norm_gain, expert_weights, slot_expert, pair_slots, combine_weights)

    return layer
```

```python
import jax
import jax.numpy as jnp
from jax import lax
from jax.sharding import Mesh, PartitionSpec as P

SWAP = [(0, 1), (1, 0)]
CROSS = [(0, 3), (1, 2), (2, 1), (3, 0)]


def normalize(tokens, norm_gain):
    values = tokens.astype(jnp.float32)
    mean_square = jnp.mean(values * values, axis=1, keepdims=True)
    return (values * lax.rsqrt(mean_square + 1e-06) * norm_gain[None, :]).astype(jnp.bfloat16)


def in_order(bit, near, far, axis):
    return jnp.where(
        bit == 0, jnp.concatenate([near, far], axis=axis), jnp.concatenate([far, near], axis=axis)
    )


def slot_coefficients(slot_expert, pair_slots, combine_weights, experts):
    slots = jnp.arange(slot_expert.shape[0], dtype=jnp.int32)
    held = slot_expert[None, None, :]
    chosen = jnp.sum(jnp.where(pair_slots[:, :, None] == slots[None, None, :], held, 0), axis=2)
    numbers = jnp.arange(experts, dtype=jnp.int32)
    weights = combine_weights[:, :, None]
    return jnp.sum(jnp.where(chosen[:, :, None] == numbers[None, None, :], weights, 0.0), axis=1)


def exchange(value, axes):
    return lax.all_to_all(value, axes, 0, 0, tiled=True)


def dense_layer(tokens, norm_gain, expert_weights, slot_expert, pair_slots, combine_weights):
    experts, own_rows, packed = expert_weights.shape
    token_count, width = tokens.shape
    hidden_units = packed // 3
    part = hidden_units // 2
    chip_axes = ("z", "y", "x")
    chips = experts
    h, c = lax.axis_index("h"), lax.axis_index("c")
    chip = lax.axis_index(chip_axes)
    group = lax.axis_size("x") * own_rows
    groups = width // (2 * group)

    gate, up, own_down = (expert_weights[:, :, i * hidden_units :][:, :, :hidden_units] for i in range(3))
    blocks = [
        jnp.concatenate([gate[:, :, i * part :][:, :, :part], up[:, :, i * part :][:, :, :part]], axis=2)
        for i in range(2)
    ]
    gate_up = exchange(jnp.concatenate(blocks), ("h",) + chip_axes)
    gate_up = gate_up.reshape(width // 2, 2 * part)
    down = exchange(own_down, chip_axes).reshape(width // 4, hidden_units)

    normed = normalize(tokens, norm_gain)
    columns = [
        jnp.concatenate([normed[:, (2 * g + j) * group :][:, :group] for g in range(groups)], axis=1)
        for j in range(2)
    ]
    keep = jnp.where(c == 0, columns[0], columns[1])
    give = jnp.where(c == 0, columns[1], columns[0])
    from_c = lax.ppermute(give, "c", SWAP)
    from_h = lax.ppermute(keep, "h", SWAP)
    from_hc = lax.ppermute(give, ("h", "c"), CROSS)
    near = jnp.concatenate(
        [in_order(h, keep[None], from_h[None], 0), in_order(h, from_c[None], from_hc[None], 0)]
    )
    rows = jnp.zeros((4, chips * token_count, width // 2), near.dtype)
    rows = lax.dynamic_update_slice(rows, near, (0, chip * token_count, 0))
    for step in range(1, chips):
        pairs = [(i, i ^ step) for i in range(chips)]
        arrived = lax.ppermute(near, chip_axes, pairs)
        rows = lax.dynamic_update_slice(rows, arrived, (0, (chip ^ step) * token_count, 0))
    count = 2 * chips * token_count
    rows = rows.reshape(2, count, width // 2)

    other = jnp.dot(rows[1], gate_up, preferred_element_type=jnp.float32).astype(jnp.bfloat16)
    arrived = lax.ppermute(other, "c", SWAP)
    pre = jnp.dot(rows[0], gate_up, preferred_element_type=jnp.float32) + arrived.astype(jnp.float32)
    hidden = (jax.nn.silu(pre[:, :part]) * pre[:, part:]).astype(jnp.bfloat16)
    hidden = in_order(h, hidden, lax.ppermute(hidden, "h", SWAP), 1)
    hidden = in_order(c, hidden, lax.ppermute(hidden, "c", SWAP), 0)
    result = lax.dot_general(hidden, down, (((1,), (1,)), ((), ())), preferred_element_type=jnp.float32)
    result = result.astype(jnp.bfloat16).reshape(4 * chips, token_count, width // 4)
    returned = exchange(result, ("c", "h") + chip_axes)
    returned = returned.reshape(2, 2, chips, token_count, width // 4).astype(jnp.float32)
    coefficient = slot_coefficients(slot_expert, pair_slots, combine_weights, experts)
    mixed = jnp.sum(returned * coefficient.T[None, None, :, :, None], axis=2).astype(jnp.bfloat16)
    spans = [
        mixed[j, i, :, g * group : (g + 1) * group] for i in range(2) for g in range(groups // 2) for j in range(2)
    ]
    return jnp.concatenate(spans, axis=1)


def per_device(tokens, norm_gain, expert_weights, slot_expert, pair_slots, combine_weights):
    slot_count = lax.axis_size("dp")
    model_width = tokens.shape[1]
    packed_width = expert_weights.shape[2]
    hidden_units = packed_width // 3
    token_count = tokens.shape[0]
    choice_count = pair_slots.shape[1]
    pair_count = token_count * choice_count
    capacity = max(2, 2 * pair_count // slot_count)
    outgoing = jnp.take(expert_weights, slot_expert, axis=0)
    arrived = lax.all_to_all(outgoing, "dp", split_axis=0, concat_axis=0, tiled=True)
    assembled = lax.all_gather(arrived[:, None], "rep", axis=1, tiled=True)
    weight = assembled.reshape(model_width, packed_width)
    values = tokens.astype(jnp.float32)
    mean_square = jnp.mean(values * values, axis=1, keepdims=True)
    normed = (values * lax.rsqrt(mean_square + 1e-06) * norm_gain[None, :]).astype(jnp.bfloat16)
    targets = pair_slots.reshape(pair_count)
    onehot = (targets[:, None] == jnp.arange(slot_count, dtype=jnp.int32)[None, :]).astype(
        jnp.int32
    )
    before = jnp.cumsum(onehot, axis=0) - onehot
    position = jnp.sum(before * onehot, axis=1)
    target_row = targets * capacity + position
    selector = (
        jnp.arange(slot_count * capacity, dtype=jnp.int32)[:, None] == target_row[None, :]
    ).astype(jnp.bfloat16)
    pair_rows = jnp.repeat(normed, choice_count, axis=0)
    outbound = jnp.dot(selector, pair_rows, preferred_element_type=jnp.float32).astype(jnp.bfloat16)
    outbound = outbound.reshape(slot_count, capacity, model_width)
    rows = lax.all_to_all(outbound, "dp", split_axis=0, concat_axis=0, tiled=True).reshape(
        -1, model_width
    )
    gate_up = jnp.dot(rows, weight[:, : 2 * hidden_units], preferred_element_type=jnp.float32)
    hidden = (jax.nn.silu(gate_up[:, :hidden_units]) * gate_up[:, hidden_units:]).astype(
        jnp.bfloat16
    )
    result = lax.dot_general(
        hidden,
        weight[:, 2 * hidden_units :],
        (((1,), (1,)), ((), ())),
        preferred_element_type=jnp.float32,
    )
    result = result.astype(jnp.bfloat16).reshape(slot_count, -1, model_width)
    returned = lax.all_to_all(result, "dp", split_axis=0, concat_axis=0, tiled=True)
    expert_out = jnp.dot(
        selector.T,
        returned.reshape(slot_count * capacity, model_width),
        preferred_element_type=jnp.float32,
    )
    expert_out = expert_out.reshape(token_count, choice_count, model_width)
    mixed = jnp.sum(expert_out * combine_weights[:, :, None], axis=1)
    return mixed.astype(jnp.bfloat16)


def solution(mesh):
    slots, engines = mesh.shape["dp"], mesh.shape["rep"]

    def layer(tokens, norm_gain, expert_weights, slot_expert, pair_slots, combine_weights):
        experts = expert_weights.shape[0]
        dense = engines == 2 and slots == 2 * experts and slots % 8 == 0 and slots <= 16
        if dense:
            devices = mesh.devices.reshape(2, slots // 8, 2, 2, engines)
            inner, split = Mesh(devices, ("h", "z", "y", "c", "x")), ("h", "z", "y", "c", "x")
        else:
            inner, split = mesh, ("dp", "rep")
        placed = (P(split, None), P(), P(None, split, None), P(), P(split, None), P(split, None))
        return jax.shard_map(
            dense_layer if dense else per_device,
            mesh=inner,
            in_specs=placed,
            out_specs=P(split, None),
            check_vma=False,
        )(tokens, norm_gain, expert_weights, slot_expert, pair_slots, combine_weights)

    return layer
```

```python
import jax
import jax.numpy as jnp
from jax import lax
from jax.experimental import pallas as pl
from jax.experimental.pallas import tpu as pltpu
from jax.sharding import Mesh, PartitionSpec as P

SWAP = [(0, 1), (1, 0)]
PACK_STEPS = 4
CROSS = [(0, 3), (1, 2), (2, 1), (3, 0)]


def normalize(tokens, norm_gain):
    values = tokens.astype(jnp.float32)
    mean_square = jnp.mean(values * values, axis=1, keepdims=True)
    return (values * lax.rsqrt(mean_square + 1e-06) * norm_gain[None, :]).astype(jnp.bfloat16)


def in_order(bit, near, far, axis):
    return jnp.where(
        bit == 0, jnp.concatenate([near, far], axis=axis), jnp.concatenate([far, near], axis=axis)
    )


def slot_coefficients(slot_expert, pair_slots, combine_weights, experts):
    slots = jnp.arange(slot_expert.shape[0], dtype=jnp.int32)
    held = slot_expert[None, None, :]
    chosen = jnp.sum(jnp.where(pair_slots[:, :, None] == slots[None, None, :], held, 0), axis=2)
    numbers = jnp.arange(experts, dtype=jnp.int32)
    weights = combine_weights[:, :, None]
    return jnp.sum(jnp.where(chosen[:, :, None] == numbers[None, None, :], weights, 0.0), axis=1)


def exchange(value, axes):
    return lax.all_to_all(value, axes, 0, 0, tiled=True)


def pack_kernel(weights, packed):
    hidden_units = packed.shape[-1]
    part = hidden_units // 2
    for i in range(2):
        packed[i, :, :, :part] = weights[:, :, i * part : (i + 1) * part]
        packed[i, :, :, part:] = weights[:, :, hidden_units + i * part : hidden_units + (i + 1) * part]


def pack(weights, hidden_units):
    experts, rows, _ = weights.shape
    step = experts // PACK_STEPS
    return pl.pallas_call(
        pack_kernel,
        name="pack",
        grid=(PACK_STEPS,),
        in_specs=[pl.BlockSpec((step, rows, 2 * hidden_units), lambda k: (k, 0, 0))],
        out_specs=pl.BlockSpec((2, step, rows, hidden_units), lambda k: (0, k, 0, 0)),
        out_shape=jax.ShapeDtypeStruct((2, experts, rows, hidden_units), weights.dtype),
    )(weights)


def gather_kernel(place, *refs):
    *blocks, out, arrived = refs
    rows = blocks[0].shape[1]
    copies = []
    for step, block in enumerate(blocks):
        target = out.at[pl.ds((place[0] ^ step) * rows, rows)]
        copies.append(pltpu.make_async_copy(block.at[0], target, arrived.at[step]))
        copies[-1].start()
    for copy in copies:
        copy.wait()


def gather_blocks(chip, blocks):
    _, rows, columns = blocks[0].shape
    return pl.pallas_call(
        gather_kernel,
        name="gather_blocks",
        in_specs=[pl.BlockSpec(memory_space=pltpu.SMEM)]
        + [pl.BlockSpec(memory_space=pltpu.HBM)] * len(blocks),
        out_specs=pl.BlockSpec(memory_space=pltpu.VMEM),
        out_shape=jax.ShapeDtypeStruct((len(blocks) * rows, columns), blocks[0].dtype),
        scratch_shapes=[pltpu.SemaphoreType.DMA((len(blocks),))],
    )(chip.reshape(1).astype(jnp.int32), *blocks)


def dense_layer(tokens, norm_gain, expert_weights, slot_expert, pair_slots, combine_weights):
    experts, own_rows, packed = expert_weights.shape
    token_count, width = tokens.shape
    hidden_units = packed // 3
    part = hidden_units // 2
    chip_axes = ("z", "y", "x")
    chips = experts
    h, c = lax.axis_index("h"), lax.axis_index("c")
    chip = lax.axis_index(chip_axes)
    group = lax.axis_size("x") * own_rows
    groups = width // (2 * group)

    gate_up = pack(expert_weights, hidden_units)
    gate_up = exchange(gate_up.reshape(2 * experts, own_rows, 2 * part), ("h",) + chip_axes)
    gate_up = gate_up.reshape(width // 2, 2 * part)
    own_down = expert_weights[:, :, 2 * hidden_units :]
    down = [lax.dynamic_slice_in_dim(own_down, chip ^ step, 1, 0) for step in range(chips)]
    for step in range(1, chips):
        down[step] = lax.ppermute(down[step], chip_axes, [(i, i ^ step) for i in range(chips)])
    down = gather_blocks(chip, down)

    normed = normalize(tokens, norm_gain)
    columns = [
        jnp.concatenate([normed[:, (2 * g + j) * group :][:, :group] for g in range(groups)], axis=1)
        for j in range(2)
    ]
    keep = jnp.where(c == 0, columns[0], columns[1])
    give = jnp.where(c == 0, columns[1], columns[0])
    from_c = lax.ppermute(give, "c", SWAP)
    from_h = lax.ppermute(keep, "h", SWAP)
    from_hc = lax.ppermute(give, ("h", "c"), CROSS)
    near = jnp.stack([in_order(h, keep, from_h, 0), in_order(h, from_c, from_hc, 0)])
    z, plane = lax.axis_index("z"), lax.axis_index(("y", "x"))
    column = in_order(z, near[:, None], lax.ppermute(near, "z", SWAP)[:, None], 1)
    rows = jnp.zeros((2, 2, chips // 2, 2 * token_count, width // 2), near.dtype)
    rows = lax.dynamic_update_slice(rows, column[:, :, None], (0, 0, plane, 0, 0))
    for step in range(1, chips // 2):
        pairs = [(i, i ^ step) for i in range(chips // 2)]
        arrived = lax.ppermute(column, ("y", "x"), pairs)
        rows = lax.dynamic_update_slice(rows, arrived[:, :, None], (0, 0, plane ^ step, 0, 0))
    count = chips * token_count
    rows = rows.reshape(2, 1, 2 * count, width // 2)

    other = jnp.dot(rows[1, 0], gate_up, preferred_element_type=jnp.float32).astype(jnp.bfloat16)
    arrived = lax.ppermute(other, "c", SWAP)
    pre = jnp.dot(rows[0, 0], gate_up, preferred_element_type=jnp.float32) + arrived.astype(jnp.float32)
    hidden = (jax.nn.silu(pre[:, :part]) * pre[:, part:]).astype(jnp.bfloat16)
    far = lax.ppermute(hidden, "h", SWAP)
    coefficient = slot_coefficients(slot_expert, pair_slots, combine_weights, experts).T
    far_weights = lax.ppermute(coefficient, "h", SWAP)
    far, far_weights = lax.optimization_barrier((far, far_weights))
    near_weights = in_order(h, coefficient, far_weights, 1)
    coefficient = in_order(c, near_weights, lax.ppermute(near_weights, "c", SWAP), 1)
    hidden = in_order(h, hidden, far, 1).reshape(chips, 2 * token_count, hidden_units)
    hidden = in_order(c, hidden, lax.ppermute(hidden, "c", SWAP), 1)
    hidden = hidden.reshape(2 * count * 2, hidden_units)
    result = lax.dot_general(hidden, down, (((1,), (1,)), ((), ())), preferred_element_type=jnp.float32)
    result = result.astype(jnp.bfloat16).reshape(chips, 4 * token_count, width // 4)
    returned = exchange(result, chip_axes).astype(jnp.float32)
    mixed = jnp.sum(returned * coefficient[:, :, None], axis=0).astype(jnp.bfloat16)
    mixed = mixed.reshape(2, 2, token_count, width // 4)

    def owned(j, i):
        first, second = jnp.where(i == 0, mixed[0, 0], mixed[0, 1]), jnp.where(i == 0, mixed[1, 0], mixed[1, 1])
        return jnp.where(j == 0, first, second)

    from_h = lax.ppermute(owned(c, 1 - h), "h", SWAP)
    from_hc = lax.ppermute(owned(1 - c, 1 - h), ("h", "c"), CROSS)
    from_c = lax.ppermute(owned(1 - c, h), "c", SWAP)
    mine = in_order(h, owned(c, h), from_h, 1)
    theirs = in_order(h, from_c, from_hc, 1)
    even, odd = jnp.where(c == 0, mine, theirs), jnp.where(c == 0, theirs, mine)
    spans = [side[:, g * group : (g + 1) * group] for g in range(groups) for side in (even, odd)]
    return jnp.concatenate(spans, axis=1)


def per_device(tokens, norm_gain, expert_weights, slot_expert, pair_slots, combine_weights):
    slot_count = lax.axis_size("dp")
    model_width = tokens.shape[1]
    packed_width = expert_weights.shape[2]
    hidden_units = packed_width // 3
    token_count = tokens.shape[0]
    choice_count = pair_slots.shape[1]
    pair_count = token_count * choice_count
    capacity = max(2, 2 * pair_count // slot_count)
    outgoing = jnp.take(expert_weights, slot_expert, axis=0)
    arrived = lax.all_to_all(outgoing, "dp", split_axis=0, concat_axis=0, tiled=True)
    assembled = lax.all_gather(arrived[:, None], "rep", axis=1, tiled=True)
    weight = assembled.reshape(model_width, packed_width)
    values = tokens.astype(jnp.float32)
    mean_square = jnp.mean(values * values, axis=1, keepdims=True)
    normed = (values * lax.rsqrt(mean_square + 1e-06) * norm_gain[None, :]).astype(jnp.bfloat16)
    targets = pair_slots.reshape(pair_count)
    onehot = (targets[:, None] == jnp.arange(slot_count, dtype=jnp.int32)[None, :]).astype(
        jnp.int32
    )
    before = jnp.cumsum(onehot, axis=0) - onehot
    position = jnp.sum(before * onehot, axis=1)
    target_row = targets * capacity + position
    selector = (
        jnp.arange(slot_count * capacity, dtype=jnp.int32)[:, None] == target_row[None, :]
    ).astype(jnp.bfloat16)
    pair_rows = jnp.repeat(normed, choice_count, axis=0)
    outbound = jnp.dot(selector, pair_rows, preferred_element_type=jnp.float32).astype(jnp.bfloat16)
    outbound = outbound.reshape(slot_count, capacity, model_width)
    rows = lax.all_to_all(outbound, "dp", split_axis=0, concat_axis=0, tiled=True).reshape(
        -1, model_width
    )
    gate_up = jnp.dot(rows, weight[:, : 2 * hidden_units], preferred_element_type=jnp.float32)
    hidden = (jax.nn.silu(gate_up[:, :hidden_units]) * gate_up[:, hidden_units:]).astype(
        jnp.bfloat16
    )
    result = lax.dot_general(
        hidden,
        weight[:, 2 * hidden_units :],
        (((1,), (1,)), ((), ())),
        preferred_element_type=jnp.float32,
    )
    result = result.astype(jnp.bfloat16).reshape(slot_count, -1, model_width)
    returned = lax.all_to_all(result, "dp", split_axis=0, concat_axis=0, tiled=True)
    expert_out = jnp.dot(
        selector.T,
        returned.reshape(slot_count * capacity, model_width),
        preferred_element_type=jnp.float32,
    )
    expert_out = expert_out.reshape(token_count, choice_count, model_width)
    mixed = jnp.sum(expert_out * combine_weights[:, :, None], axis=1)
    return mixed.astype(jnp.bfloat16)


def solution(mesh):
    slots, engines = mesh.shape["dp"], mesh.shape["rep"]

    def layer(tokens, norm_gain, expert_weights, slot_expert, pair_slots, combine_weights):
        experts = expert_weights.shape[0]
        dense = engines == 2 and slots == 2 * experts and slots % 8 == 0 and slots <= 16
        if dense:
            devices = mesh.devices.reshape(2, slots // 8, 2, 2, engines)
            inner, split = Mesh(devices, ("h", "z", "y", "c", "x")), ("h", "z", "y", "c", "x")
        else:
            inner, split = mesh, ("dp", "rep")
        placed = (P(split, None), P(), P(None, split, None), P(), P(split, None), P(split, None))
        return jax.shard_map(
            dense_layer if dense else per_device,
            mesh=inner,
            in_specs=placed,
            out_specs=P(split, None),
            check_vma=False,
        )(tokens, norm_gain, expert_weights, slot_expert, pair_slots, combine_weights)

    return layer
```

```python
import functools

import jax
import jax.numpy as jnp
from jax import lax
from jax.experimental import pallas as pl
from jax.experimental.pallas import tpu as pltpu
from jax.sharding import Mesh, PartitionSpec as P

SWAP = [(0, 1), (1, 0)]
PACK_STEPS = 4
LIMIT = 61 * 2**20
CROSS = [(0, 3), (1, 2), (2, 1), (3, 0)]


def in_order(bit, near, far, axis):
    return jnp.where(
        bit == 0, jnp.concatenate([near, far], axis=axis), jnp.concatenate([far, near], axis=axis)
    )


def slot_coefficients(slot_expert, pair_slots, combine_weights, experts):
    slots = jnp.arange(slot_expert.shape[0], dtype=jnp.int32)
    held = slot_expert[None, None, :]
    chosen = jnp.sum(jnp.where(pair_slots[:, :, None] == slots[None, None, :], held, 0), axis=2)
    numbers = jnp.arange(experts, dtype=jnp.int32)
    weights = combine_weights[:, :, None]
    return jnp.sum(jnp.where(chosen[:, :, None] == numbers[None, None, :], weights, 0.0), axis=1)


def assemble_kernel(group, half, mine, other, out):
    cores, _, columns = mine.shape

    def write(first, second):
        for i, side in enumerate((first, second)):
            for g in range(columns // group):
                for j in range(cores):
                    start = ((i * (columns // group) + g) * cores + j) * group
                    out[:, start : start + group] = side[j, :, g * group : (g + 1) * group]

    @pl.when(half[0] == 0)
    def _():
        write(mine, other)

    @pl.when(half[0] != 0)
    def _():
        write(other, mine)


def assemble(half, mine, other, group):
    cores, rows, columns = mine.shape
    vmem = pl.BlockSpec(memory_space=pltpu.VMEM)
    return pl.pallas_call(
        functools.partial(assemble_kernel, group),
        name="assemble",
        in_specs=[pl.BlockSpec(memory_space=pltpu.SMEM), vmem, vmem],
        out_specs=vmem,
        out_shape=jax.ShapeDtypeStruct((rows, 2 * cores * columns), mine.dtype),
        compiler_params=pltpu.CompilerParams(vmem_limit_bytes=2**20),
    )(half.reshape(1).astype(jnp.int32), mine, other)


def exchange(value, axes):
    return lax.all_to_all(value, axes, 0, 0, tiled=True)


def prepare_kernel(groups, core, plane, all_tokens, all_gain, weights, keep, give, packed, *refs):
    *blocks, tokens, gain, first, ready = refs
    loads = [
        pltpu.make_async_copy(all_tokens, tokens, first.at[0]),
        pltpu.make_async_copy(all_gain, gain, first.at[1]),
    ]
    for load in loads:
        load.start()
    experts, _, packed_width = weights.shape
    hidden_units = packed_width // 3
    part, places = hidden_units // 2, len(blocks)
    copies = []

    def copy(source, target):
        copies.append(pltpu.make_async_copy(source, target, ready.at[len(copies)]))
        copies[-1].start()

    size = experts // PACK_STEPS
    for k in range(PACK_STEPS):
        some = pl.ds(k * size, size)
        for i in range(2):
            for j in range(2):
                source = weights.at[some, :, pl.ds(j * hidden_units + i * part, part)]
                copy(source, packed.at[i, some, :, pl.ds(j * part, part)])
    for step, block in enumerate(blocks):
        for level in range(experts // places):
            expert = level * places + (plane[0] ^ step)
            copy(weights.at[expert, :, pl.ds(2 * hidden_units, hidden_units)], block.at[level])

    for load in loads:
        load.wait()
    values = tokens[...].astype(jnp.float32)
    mean_square = jnp.mean(values * values, axis=1, keepdims=True)
    normed = (values * lax.rsqrt(mean_square + 1e-06) * gain[...]).astype(keep.dtype)
    group = normed.shape[1] // 2 // groups

    def split(first, second):
        for g in range(groups):
            at = slice(g * group, (g + 1) * group)
            first[:, at] = normed[:, 2 * g * group : (2 * g + 1) * group]
            second[:, at] = normed[:, (2 * g + 1) * group : (2 * g + 2) * group]

    @pl.when(core[0] == 0)
    def _():
        split(keep, give)

    @pl.when(core[0] != 0)
    def _():
        split(give, keep)

    for started in copies:
        started.wait()


def prepare(core, plane, tokens, gain, weights, groups):
    experts, rows, packed_width = weights.shape
    count, width = tokens.shape
    hidden_units = packed_width // 3
    places = experts // 2
    scalar, vmem = pl.BlockSpec(memory_space=pltpu.SMEM), pl.BlockSpec(memory_space=pltpu.VMEM)
    hbm = pl.BlockSpec(memory_space=pltpu.HBM)
    columns = jax.ShapeDtypeStruct((count, width // 2), tokens.dtype)
    block = jax.ShapeDtypeStruct((2, rows, hidden_units), weights.dtype)
    packed = jax.ShapeDtypeStruct((2, experts, rows, hidden_units), weights.dtype)
    return pl.pallas_call(
        functools.partial(prepare_kernel, groups),
        name="prepare",
        in_specs=[scalar, scalar, hbm, hbm, hbm],
        out_specs=[vmem] * (3 + places),
        out_shape=[columns, columns, packed] + [block] * places,
        scratch_shapes=[
            pltpu.VMEM((count, width), tokens.dtype),
            pltpu.VMEM((1, width), gain.dtype),
            pltpu.SemaphoreType.DMA((2,)),
            pltpu.SemaphoreType.DMA((4 * PACK_STEPS + experts,)),
        ],
        compiler_params=pltpu.CompilerParams(vmem_limit_bytes=LIMIT),
    )(core.reshape(1), plane.reshape(1), tokens, gain.reshape(1, width), weights)


def gather_kernel(level, plane, kept, arrived, out, ready):
    copies = []
    for i, blocks in enumerate((kept, arrived)):
        for step in range(blocks.shape[0]):
            target = out.at[level[0] ^ i, plane[0] ^ step]
            copies.append(pltpu.make_async_copy(blocks.at[step], target, ready.at[i, step]))
            copies[-1].start()
    for copy in copies:
        copy.wait()


def gather_blocks(level, plane, kept, arrived):
    scalar, hbm = pl.BlockSpec(memory_space=pltpu.SMEM), pl.BlockSpec(memory_space=pltpu.HBM)
    return pl.pallas_call(
        gather_kernel,
        name="gather_blocks",
        in_specs=[scalar, scalar, hbm, hbm],
        out_specs=pl.BlockSpec(memory_space=pltpu.VMEM),
        out_shape=jax.ShapeDtypeStruct((2,) + kept.shape, kept.dtype),
        scratch_shapes=[pltpu.SemaphoreType.DMA((2, kept.shape[0]))],
        compiler_params=pltpu.CompilerParams(vmem_limit_bytes=2**21),
    )(level.reshape(1), plane.reshape(1), kept, arrived)


def dense_layer(tokens, norm_gain, expert_weights, slot_expert, pair_slots, combine_weights):
    experts, own_rows, packed = expert_weights.shape
    token_count, width = tokens.shape
    hidden_units = packed // 3
    part = hidden_units // 2
    chip_axes = ("z", "y", "x")
    chips = experts
    h, c = lax.axis_index("h"), lax.axis_index("c")
    group = lax.axis_size("x") * own_rows
    groups = width // (2 * group)

    z, plane = lax.axis_index("z"), lax.axis_index(("y", "x"))
    places = chips // 2
    keep, give, packed, *blocks = prepare(c, plane, tokens, norm_gain, expert_weights, groups)
    gate_up = exchange(packed.reshape(2 * experts, own_rows, 2 * part), ("h",) + chip_axes)
    gate_up = gate_up.reshape(width // 2, 2 * part)

    for step in range(1, places):
        pairs = [(i, i ^ step) for i in range(places)]
        blocks[step] = lax.ppermute(blocks[step], ("y", "x"), pairs)
    kept = jnp.stack([lax.dynamic_index_in_dim(block, z, 0, keepdims=False) for block in blocks])
    passed = jnp.stack([lax.dynamic_index_in_dim(block, 1 - z, 0, keepdims=False) for block in blocks])
    down = gather_blocks(z, plane, kept, lax.ppermute(passed, "z", SWAP))
    down = down.reshape(width // 4, hidden_units)

    from_c = lax.ppermute(give, "c", SWAP)
    from_h = lax.ppermute(keep, "h", SWAP)
    from_hc = lax.ppermute(give, ("h", "c"), CROSS)
    near = jnp.stack([in_order(h, keep, from_h, 0), in_order(h, from_c, from_hc, 0)])
    column = in_order(z, near[:, None], lax.ppermute(near, "z", SWAP)[:, None], 1)
    rows = jnp.zeros((2, 2, chips // 2, 2 * token_count, width // 2), near.dtype)
    rows = lax.dynamic_update_slice(rows, column[:, :, None], (0, 0, plane, 0, 0))
    for step in range(1, chips // 2):
        pairs = [(i, i ^ step) for i in range(chips // 2)]
        arrived = lax.ppermute(column, ("y", "x"), pairs)
        rows = lax.dynamic_update_slice(rows, arrived[:, :, None], (0, 0, plane ^ step, 0, 0))
    count = chips * token_count
    rows = rows.reshape(2, 1, 2 * count, width // 2)

    other = jnp.dot(rows[1, 0], gate_up, preferred_element_type=jnp.float32).astype(jnp.bfloat16)
    arrived = lax.ppermute(other, "c", SWAP)
    pre = jnp.dot(rows[0, 0], gate_up, preferred_element_type=jnp.float32) + arrived.astype(jnp.float32)
    hidden = (jax.nn.silu(pre[:, :part]) * pre[:, part:]).astype(jnp.bfloat16)
    far = lax.ppermute(hidden, "h", SWAP)
    coefficient = slot_coefficients(slot_expert, pair_slots, combine_weights, experts).T
    far_weights = lax.ppermute(coefficient, "h", SWAP)
    far, far_weights = lax.optimization_barrier((far, far_weights))
    coefficient = in_order(h, coefficient, far_weights, 1)
    hidden = in_order(h, hidden, far, 1)
    hidden = in_order(c, hidden, lax.ppermute(hidden, "c", SWAP), 0)
    hidden = lax.optimization_barrier(hidden)
    result = lax.dot_general(hidden, down, (((1,), (1,)), ((), ())), preferred_element_type=jnp.float32)
    result = result.astype(jnp.bfloat16).reshape(2 * chips, 2 * token_count, width // 4)
    returned = exchange(result, ("c",) + chip_axes).astype(jnp.float32)
    returned = returned.reshape(2, chips, 2 * token_count, width // 4)
    mixed = jnp.sum(returned * coefficient[None, :, :, None], axis=1).astype(jnp.bfloat16)
    low, high = mixed[:, :token_count], mixed[:, token_count:]
    mine, sent = jnp.where(h == 0, low, high), jnp.where(h == 0, high, low)
    return assemble(h, mine, lax.ppermute(sent, "h", SWAP), group)


def per_device(tokens, norm_gain, expert_weights, slot_expert, pair_slots, combine_weights):
    slot_count = lax.axis_size("dp")
    model_width = tokens.shape[1]
    packed_width = expert_weights.shape[2]
    hidden_units = packed_width // 3
    token_count = tokens.shape[0]
    choice_count = pair_slots.shape[1]
    pair_count = token_count * choice_count
    capacity = max(2, 2 * pair_count // slot_count)
    outgoing = jnp.take(expert_weights, slot_expert, axis=0)
    arrived = lax.all_to_all(outgoing, "dp", split_axis=0, concat_axis=0, tiled=True)
    assembled = lax.all_gather(arrived[:, None], "rep", axis=1, tiled=True)
    weight = assembled.reshape(model_width, packed_width)
    values = tokens.astype(jnp.float32)
    mean_square = jnp.mean(values * values, axis=1, keepdims=True)
    normed = (values * lax.rsqrt(mean_square + 1e-06) * norm_gain[None, :]).astype(jnp.bfloat16)
    targets = pair_slots.reshape(pair_count)
    onehot = (targets[:, None] == jnp.arange(slot_count, dtype=jnp.int32)[None, :]).astype(
        jnp.int32
    )
    before = jnp.cumsum(onehot, axis=0) - onehot
    position = jnp.sum(before * onehot, axis=1)
    target_row = targets * capacity + position
    selector = (
        jnp.arange(slot_count * capacity, dtype=jnp.int32)[:, None] == target_row[None, :]
    ).astype(jnp.bfloat16)
    pair_rows = jnp.repeat(normed, choice_count, axis=0)
    outbound = jnp.dot(selector, pair_rows, preferred_element_type=jnp.float32).astype(jnp.bfloat16)
    outbound = outbound.reshape(slot_count, capacity, model_width)
    rows = lax.all_to_all(outbound, "dp", split_axis=0, concat_axis=0, tiled=True).reshape(
        -1, model_width
    )
    gate_up = jnp.dot(rows, weight[:, : 2 * hidden_units], preferred_element_type=jnp.float32)
    hidden = (jax.nn.silu(gate_up[:, :hidden_units]) * gate_up[:, hidden_units:]).astype(
        jnp.bfloat16
    )
    result = lax.dot_general(
        hidden,
        weight[:, 2 * hidden_units :],
        (((1,), (1,)), ((), ())),
        preferred_element_type=jnp.float32,
    )
    result = result.astype(jnp.bfloat16).reshape(slot_count, -1, model_width)
    returned = lax.all_to_all(result, "dp", split_axis=0, concat_axis=0, tiled=True)
    expert_out = jnp.dot(
        selector.T,
        returned.reshape(slot_count * capacity, model_width),
        preferred_element_type=jnp.float32,
    )
    expert_out = expert_out.reshape(token_count, choice_count, model_width)
    mixed = jnp.sum(expert_out * combine_weights[:, :, None], axis=1)
    return mixed.astype(jnp.bfloat16)


def solution(mesh):
    slots, engines = mesh.shape["dp"], mesh.shape["rep"]

    def layer(tokens, norm_gain, expert_weights, slot_expert, pair_slots, combine_weights):
        experts = expert_weights.shape[0]
        dense = engines == 2 and slots == 2 * experts and slots % 8 == 0 and slots <= 16
        if dense:
            devices = mesh.devices.reshape(2, slots // 8, 2, 2, engines)
            inner, split = Mesh(devices, ("h", "z", "y", "c", "x")), ("h", "z", "y", "c", "x")
        else:
            inner, split = mesh, ("dp", "rep")
        placed = (P(split, None), P(), P(None, split, None), P(), P(split, None), P(split, None))
        return jax.shard_map(
            dense_layer if dense else per_device,
            mesh=inner,
            in_specs=placed,
            out_specs=P(split, None),
            check_vma=False,
        )(tokens, norm_gain, expert_weights, slot_expert, pair_slots, combine_weights)

    return layer
```

```python
import functools

import jax
import jax.numpy as jnp
from jax import lax
from jax.experimental import pallas as pl
from jax.experimental.pallas import tpu as pltpu
from jax.sharding import Mesh, PartitionSpec as P

SWAP = [(0, 1), (1, 0)]
PACK_STEPS = 4
LIMIT = 61 * 2**20
CROSS = [(0, 3), (1, 2), (2, 1), (3, 0)]


def in_order(bit, near, far, axis):
    return jnp.where(
        bit == 0, jnp.concatenate([near, far], axis=axis), jnp.concatenate([far, near], axis=axis)
    )


def slot_coefficients(slot_expert, pair_slots, combine_weights, experts):
    slots = jnp.arange(slot_expert.shape[0], dtype=jnp.int32)
    held = slot_expert[None, None, :]
    chosen = jnp.sum(jnp.where(pair_slots[:, :, None] == slots[None, None, :], held, 0), axis=2)
    numbers = jnp.arange(experts, dtype=jnp.int32)
    weights = combine_weights[:, :, None]
    return jnp.sum(jnp.where(chosen[:, :, None] == numbers[None, None, :], weights, 0.0), axis=1)


def assemble_kernel(half, mine, other, out):
    columns = mine.shape[1]
    own = pl.multiple_of(half[0] * columns, columns)
    out[:, pl.ds(own, columns)] = mine[...]
    out[:, pl.ds(columns - own, columns)] = other[...]


def assemble(half, mine, other):
    rows, columns = mine.shape
    vmem = pl.BlockSpec(memory_space=pltpu.VMEM)
    return pl.pallas_call(
        assemble_kernel,
        name="assemble",
        in_specs=[pl.BlockSpec(memory_space=pltpu.SMEM), vmem, vmem],
        out_specs=vmem,
        out_shape=jax.ShapeDtypeStruct((rows, 2 * columns), mine.dtype),
        compiler_params=pltpu.CompilerParams(vmem_limit_bytes=2**20),
    )(half.reshape(1), mine, other)


def exchange(value, axes):
    return lax.all_to_all(value, axes, 0, 0, tiled=True)


def pack_kernel(plane, weights, packed, *refs):
    *blocks, ready = refs
    experts, _, packed_width = weights.shape
    hidden_units = packed_width // 3
    part, places = hidden_units // 2, len(blocks)
    copies = []

    def copy(source, target):
        copies.append(pltpu.make_async_copy(source, target, ready.at[len(copies)]))
        copies[-1].start()

    size = experts // PACK_STEPS
    for k in range(PACK_STEPS):
        some = pl.ds(k * size, size)
        for i in range(2):
            for j in range(2):
                source = weights.at[some, :, pl.ds(j * hidden_units + i * part, part)]
                copy(source, packed.at[i, some, :, pl.ds(j * part, part)])
    for step, block in enumerate(blocks):
        for level in range(experts // places):
            expert = level * places + (plane[0] ^ step)
            copy(weights.at[expert, :, pl.ds(2 * hidden_units, hidden_units)], block.at[level])

    for started in copies:
        started.wait()


def normalize_kernel(groups, core, all_tokens, all_gain, keep, give, tokens, gain, first):
    loads = [
        pltpu.make_async_copy(all_tokens, tokens, first.at[0]),
        pltpu.make_async_copy(all_gain, gain, first.at[1]),
    ]
    for load in loads:
        load.start()
    for load in loads:
        load.wait()
    values = tokens[...].astype(jnp.float32)
    mean_square = jnp.mean(values * values, axis=1, keepdims=True)
    normed = (values * lax.rsqrt(mean_square + 1e-06) * gain[...]).astype(keep.dtype)
    group = normed.shape[1] // 2 // groups

    def split(first, second):
        for g in range(groups):
            at = slice(g * group, (g + 1) * group)
            first[:, at] = normed[:, 2 * g * group : (2 * g + 1) * group]
            second[:, at] = normed[:, (2 * g + 1) * group : (2 * g + 2) * group]

    @pl.when(core[0] == 0)
    def _():
        split(keep, give)

    @pl.when(core[0] != 0)
    def _():
        split(give, keep)


def normalize(core, tokens, gain, groups):
    count, width = tokens.shape
    hbm, vmem = pl.BlockSpec(memory_space=pltpu.HBM), pl.BlockSpec(memory_space=pltpu.VMEM)
    return pl.pallas_call(
        functools.partial(normalize_kernel, groups),
        name="normalize",
        in_specs=[pl.BlockSpec(memory_space=pltpu.SMEM), hbm, hbm],
        out_specs=[vmem] * 2,
        out_shape=[jax.ShapeDtypeStruct((count, width // 2), tokens.dtype)] * 2,
        scratch_shapes=[
            pltpu.VMEM((count, width), tokens.dtype),
            pltpu.VMEM((1, width), gain.dtype),
            pltpu.SemaphoreType.DMA((2,)),
        ],
        compiler_params=pltpu.CompilerParams(vmem_limit_bytes=LIMIT),
    )(core.reshape(1), tokens, gain.reshape(1, width))


def pack(plane, weights):
    experts, rows, packed_width = weights.shape
    hidden_units = packed_width // 3
    places = experts // 2
    vmem = pl.BlockSpec(memory_space=pltpu.VMEM)
    block = jax.ShapeDtypeStruct((2, rows, hidden_units), weights.dtype)
    packed = jax.ShapeDtypeStruct((2, experts, rows, hidden_units), weights.dtype)
    return pl.pallas_call(
        pack_kernel,
        name="pack",
        in_specs=[pl.BlockSpec(memory_space=pltpu.SMEM), pl.BlockSpec(memory_space=pltpu.HBM)],
        out_specs=[vmem] * (1 + places),
        out_shape=[packed] + [block] * places,
        scratch_shapes=[pltpu.SemaphoreType.DMA((4 * PACK_STEPS + experts,))],
        compiler_params=pltpu.CompilerParams(vmem_limit_bytes=LIMIT),
    )(plane.reshape(1), weights)


def gather_kernel(level, plane, core, *refs):
    *sources, out, ready = refs
    copies = []
    for at, blocks in enumerate(sources):
        for step in range(blocks.shape[0]):
            place = plane[0] ^ step
            target = out.at[level[0] ^ (at % 2), place // 2, core[0] ^ (at // 2), place % 2]
            copies.append(pltpu.make_async_copy(blocks.at[step], target, ready.at[at, step]))
            copies[-1].start()
    for copy in copies:
        copy.wait()


def gather_blocks(level, plane, core, sources):
    scalar, hbm = pl.BlockSpec(memory_space=pltpu.SMEM), pl.BlockSpec(memory_space=pltpu.HBM)
    places, rows, columns = sources[0].shape
    return pl.pallas_call(
        gather_kernel,
        name="gather_blocks",
        in_specs=[scalar] * 3 + [hbm] * len(sources),
        out_specs=pl.BlockSpec(memory_space=pltpu.VMEM),
        out_shape=jax.ShapeDtypeStruct((2, places // 2, 2, 2, rows, columns), sources[0].dtype),
        scratch_shapes=[pltpu.SemaphoreType.DMA((len(sources), places))],
        compiler_params=pltpu.CompilerParams(vmem_limit_bytes=3 * 2**20),
    )(level.reshape(1), plane.reshape(1), core.reshape(1), *sources)


def dense_layer(tokens, norm_gain, expert_weights, slot_expert, pair_slots, combine_weights):
    experts, own_rows, packed = expert_weights.shape
    token_count, width = tokens.shape
    hidden_units = packed // 3
    part = hidden_units // 2
    chip_axes = ("z", "y", "x")
    chips = experts
    h, c = lax.axis_index("h"), lax.axis_index("c")
    group = lax.axis_size("x") * own_rows
    groups = width // (2 * group)

    z, plane = lax.axis_index("z"), lax.axis_index(("y", "x"))
    places = chips // 2
    keep, give = normalize(c, tokens, norm_gain, groups)
    packed, *blocks = pack(plane, expert_weights)
    gate_up = exchange(packed.reshape(2 * experts, own_rows, 2 * part), ("h",) + chip_axes)
    gate_up = gate_up.reshape(width // 2, 2 * part)

    for step in range(1, places):
        pairs = [(i, i ^ step) for i in range(places)]
        blocks[step] = lax.ppermute(blocks[step], ("y", "x"), pairs)
    kept = jnp.stack([lax.dynamic_index_in_dim(block, z, 0, keepdims=False) for block in blocks])
    passed = jnp.stack([lax.dynamic_index_in_dim(block, 1 - z, 0, keepdims=False) for block in blocks])
    arrived = lax.ppermute(passed, "z", SWAP)
    sources = [kept, arrived, lax.ppermute(kept, "c", SWAP), lax.ppermute(arrived, "c", SWAP)]
    down = gather_blocks(z, plane, c, sources).reshape(width // 2, hidden_units)

    from_c = lax.ppermute(give, "c", SWAP)
    from_h = lax.ppermute(keep, "h", SWAP)
    from_hc = lax.ppermute(give, ("h", "c"), CROSS)
    near = jnp.stack([in_order(h, keep, from_h, 0), in_order(h, from_c, from_hc, 0)])
    column = in_order(z, near[:, None], lax.ppermute(near, "z", SWAP)[:, None], 1)
    rows = jnp.zeros((2, 2, chips // 2, 2 * token_count, width // 2), near.dtype)
    rows = lax.dynamic_update_slice(rows, column[:, :, None], (0, 0, plane, 0, 0))
    for step in range(1, chips // 2):
        pairs = [(i, i ^ step) for i in range(chips // 2)]
        arrived = lax.ppermute(column, ("y", "x"), pairs)
        rows = lax.dynamic_update_slice(rows, arrived[:, :, None], (0, 0, plane ^ step, 0, 0))
    count = chips * token_count
    rows = rows.reshape(2, 1, 2 * count, width // 2)

    other = jnp.dot(rows[1, 0], gate_up, preferred_element_type=jnp.float32).astype(jnp.bfloat16)
    arrived = lax.ppermute(other, "c", SWAP)
    pre = jnp.dot(rows[0, 0], gate_up, preferred_element_type=jnp.float32) + arrived.astype(jnp.float32)
    hidden = (jax.nn.silu(pre[:, :part]) * pre[:, part:]).astype(jnp.bfloat16)
    far = lax.ppermute(hidden, "h", SWAP)
    coefficient = slot_coefficients(slot_expert, pair_slots, combine_weights, experts).T
    far_weights = lax.ppermute(coefficient, "h", SWAP)
    far, far_weights = lax.optimization_barrier((far, far_weights))
    coefficient = in_order(h, coefficient, far_weights, 1)
    hidden = in_order(h, hidden, far, 1)
    hidden = lax.optimization_barrier(hidden)
    result = lax.dot_general(hidden, down, (((1,), (1,)), ((), ())), preferred_element_type=jnp.float32)
    result = result.astype(jnp.bfloat16).reshape(chips, 2 * token_count, width // 2)
    returned = exchange(result, chip_axes).astype(jnp.float32)
    mixed = jnp.sum(returned * coefficient[:, :, None], axis=0).astype(jnp.bfloat16)
    low, high = mixed[:token_count], mixed[token_count:]
    mine, sent = jnp.where(h == 0, low, high), jnp.where(h == 0, high, low)
    return assemble(h, mine, lax.ppermute(sent, "h", SWAP))


def per_device(tokens, norm_gain, expert_weights, slot_expert, pair_slots, combine_weights):
    slot_count = lax.axis_size("dp")
    model_width = tokens.shape[1]
    packed_width = expert_weights.shape[2]
    hidden_units = packed_width // 3
    token_count = tokens.shape[0]
    choice_count = pair_slots.shape[1]
    pair_count = token_count * choice_count
    capacity = max(2, 2 * pair_count // slot_count)
    outgoing = jnp.take(expert_weights, slot_expert, axis=0)
    arrived = lax.all_to_all(outgoing, "dp", split_axis=0, concat_axis=0, tiled=True)
    assembled = lax.all_gather(arrived[:, None], "rep", axis=1, tiled=True)
    weight = assembled.reshape(model_width, packed_width)
    values = tokens.astype(jnp.float32)
    mean_square = jnp.mean(values * values, axis=1, keepdims=True)
    normed = (values * lax.rsqrt(mean_square + 1e-06) * norm_gain[None, :]).astype(jnp.bfloat16)
    targets = pair_slots.reshape(pair_count)
    onehot = (targets[:, None] == jnp.arange(slot_count, dtype=jnp.int32)[None, :]).astype(
        jnp.int32
    )
    before = jnp.cumsum(onehot, axis=0) - onehot
    position = jnp.sum(before * onehot, axis=1)
    target_row = targets * capacity + position
    selector = (
        jnp.arange(slot_count * capacity, dtype=jnp.int32)[:, None] == target_row[None, :]
    ).astype(jnp.bfloat16)
    pair_rows = jnp.repeat(normed, choice_count, axis=0)
    outbound = jnp.dot(selector, pair_rows, preferred_element_type=jnp.float32).astype(jnp.bfloat16)
    outbound = outbound.reshape(slot_count, capacity, model_width)
    rows = lax.all_to_all(outbound, "dp", split_axis=0, concat_axis=0, tiled=True).reshape(
        -1, model_width
    )
    gate_up = jnp.dot(rows, weight[:, : 2 * hidden_units], preferred_element_type=jnp.float32)
    hidden = (jax.nn.silu(gate_up[:, :hidden_units]) * gate_up[:, hidden_units:]).astype(
        jnp.bfloat16
    )
    result = lax.dot_general(
        hidden,
        weight[:, 2 * hidden_units :],
        (((1,), (1,)), ((), ())),
        preferred_element_type=jnp.float32,
    )
    result = result.astype(jnp.bfloat16).reshape(slot_count, -1, model_width)
    returned = lax.all_to_all(result, "dp", split_axis=0, concat_axis=0, tiled=True)
    expert_out = jnp.dot(
        selector.T,
        returned.reshape(slot_count * capacity, model_width),
        preferred_element_type=jnp.float32,
    )
    expert_out = expert_out.reshape(token_count, choice_count, model_width)
    mixed = jnp.sum(expert_out * combine_weights[:, :, None], axis=1)
    return mixed.astype(jnp.bfloat16)


def solution(mesh):
    slots, engines = mesh.shape["dp"], mesh.shape["rep"]

    def layer(tokens, norm_gain, expert_weights, slot_expert, pair_slots, combine_weights):
        experts = expert_weights.shape[0]
        dense = engines == 2 and slots == 2 * experts and slots % 8 == 0 and slots <= 16
        if dense:
            devices = mesh.devices.reshape(2, slots // 8, 2, 2, engines)
            inner, split = Mesh(devices, ("h", "z", "y", "c", "x")), ("h", "z", "y", "c", "x")
        else:
            inner, split = mesh, ("dp", "rep")
        placed = (P(split, None), P(), P(None, split, None), P(), P(split, None), P(split, None))
        return jax.shard_map(
            dense_layer if dense else per_device,
            mesh=inner,
            in_specs=placed,
            out_specs=P(split, None),
            check_vma=False,
        )(tokens, norm_gain, expert_weights, slot_expert, pair_slots, combine_weights)

    return layer
```

```python
import functools

import jax
import jax.numpy as jnp
from jax import lax
from jax.experimental import pallas as pl
from jax.experimental.pallas import tpu as pltpu
from jax.sharding import Mesh, PartitionSpec as P

SWAP = [(0, 1), (1, 0)]
PACK_STEPS = 2
LIMIT = 61 * 2**20
CROSS = [(0, 3), (1, 2), (2, 1), (3, 0)]


def in_order(bit, near, far, axis):
    return jnp.where(
        bit == 0, jnp.concatenate([near, far], axis=axis), jnp.concatenate([far, near], axis=axis)
    )


def slot_coefficients(slot_expert, pair_slots, combine_weights, experts):
    slots = jnp.arange(slot_expert.shape[0], dtype=jnp.int32)
    held = slot_expert[None, None, :]
    chosen = jnp.sum(jnp.where(pair_slots[:, :, None] == slots[None, None, :], held, 0), axis=2)
    numbers = jnp.arange(experts, dtype=jnp.int32)
    weights = combine_weights[:, :, None]
    return jnp.sum(jnp.where(chosen[:, :, None] == numbers[None, None, :], weights, 0.0), axis=1)


def assemble_kernel(half, mine, other, out):
    columns = mine.shape[1]
    own = pl.multiple_of(half[0] * columns, columns)
    out[:, pl.ds(own, columns)] = mine[...]
    out[:, pl.ds(columns - own, columns)] = other[...]


def assemble(half, mine, other):
    rows, columns = mine.shape
    vmem = pl.BlockSpec(memory_space=pltpu.VMEM)
    return pl.pallas_call(
        assemble_kernel,
        name="assemble",
        in_specs=[pl.BlockSpec(memory_space=pltpu.SMEM), vmem, vmem],
        out_specs=vmem,
        out_shape=jax.ShapeDtypeStruct((rows, 2 * columns), mine.dtype),
        compiler_params=pltpu.CompilerParams(vmem_limit_bytes=2**20),
    )(half.reshape(1), mine, other)


def exchange(value, axes):
    return lax.all_to_all(value, axes, 0, 0, tiled=True)


def pack_kernel(plane, weights, packed, *refs):
    places = weights.shape[0] // 2
    outs, (room, down_room, ready, done) = refs[:places], refs[places:]
    experts, _, packed_width = weights.shape
    hidden_units = packed_width // 3
    part, size = hidden_units // 2, experts // PACK_STEPS
    loads, stores, at = [], [], 0

    def load(source, target):
        nonlocal at
        loads[-1].append(pltpu.make_async_copy(source, target, ready.at[at]))
        loads[-1][-1].start()
        at += 1

    for k in range(PACK_STEPS):
        some = pl.ds(k * size, size)
        for i in range(2):
            loads.append([])
            for j in range(2):
                source = weights.at[some, :, pl.ds(j * hidden_units + i * part, part)]
                load(source, room.at[i, some, :, pl.ds(j * part, part)])
            stores.append((room.at[i, some], packed.at[i, some]))
    for step in range(places):
        loads.append([])
        for level in range(2):
            expert = level * places + (plane[0] ^ step)
            load(weights.at[expert, :, pl.ds(2 * hidden_units, hidden_units)], down_room.at[step, level])
        stores.append((down_room.at[step], outs[step]))
    writes = []
    for arriving, (source, target) in zip(loads, stores, strict=True):
        for copy in arriving:
            copy.wait()
        writes.append(pltpu.make_async_copy(source, target, done.at[len(writes)]))
        writes[-1].start()
    for copy in writes:
        copy.wait()


def normalize_kernel(groups, core, all_tokens, all_gain, keep, give, tokens, gain, first):
    loads = [
        pltpu.make_async_copy(all_tokens, tokens, first.at[0]),
        pltpu.make_async_copy(all_gain, gain, first.at[1]),
    ]
    for load in loads:
        load.start()
    for load in loads:
        load.wait()
    values = tokens[...].astype(jnp.float32)
    mean_square = jnp.mean(values * values, axis=1, keepdims=True)
    normed = (values * lax.rsqrt(mean_square + 1e-06) * gain[...]).astype(keep.dtype)
    group = normed.shape[1] // 2 // groups

    def split(first, second):
        for g in range(groups):
            at = slice(g * group, (g + 1) * group)
            first[:, at] = normed[:, 2 * g * group : (2 * g + 1) * group]
            second[:, at] = normed[:, (2 * g + 1) * group : (2 * g + 2) * group]

    @pl.when(core[0] == 0)
    def _():
        split(keep, give)

    @pl.when(core[0] != 0)
    def _():
        split(give, keep)


def normalize(core, tokens, gain, groups):
    count, width = tokens.shape
    hbm, vmem = pl.BlockSpec(memory_space=pltpu.HBM), pl.BlockSpec(memory_space=pltpu.VMEM)
    return pl.pallas_call(
        functools.partial(normalize_kernel, groups),
        name="normalize",
        in_specs=[pl.BlockSpec(memory_space=pltpu.SMEM), hbm, hbm],
        out_specs=[vmem] * 2,
        out_shape=[jax.ShapeDtypeStruct((count, width // 2), tokens.dtype)] * 2,
        scratch_shapes=[
            pltpu.VMEM((count, width), tokens.dtype),
            pltpu.VMEM((1, width), gain.dtype),
            pltpu.SemaphoreType.DMA((2,)),
        ],
        compiler_params=pltpu.CompilerParams(vmem_limit_bytes=LIMIT),
    )(core.reshape(1), tokens, gain.reshape(1, width))


def pack(plane, weights):
    experts, rows, packed_width = weights.shape
    hidden_units = packed_width // 3
    places = experts // 2
    hbm = pl.BlockSpec(memory_space=pltpu.HBM)
    block = jax.ShapeDtypeStruct((2, rows, hidden_units), weights.dtype)
    packed = jax.ShapeDtypeStruct((2, experts, rows, hidden_units), weights.dtype)
    return pl.pallas_call(
        pack_kernel,
        name="pack",
        in_specs=[pl.BlockSpec(memory_space=pltpu.SMEM), hbm],
        out_specs=[hbm] * (1 + places),
        out_shape=[packed] + [block] * places,
        scratch_shapes=[
            pltpu.VMEM(packed.shape, weights.dtype),
            pltpu.VMEM((places,) + block.shape, weights.dtype),
            pltpu.SemaphoreType.DMA((4 * PACK_STEPS + experts,)),
            pltpu.SemaphoreType.DMA((2 * PACK_STEPS + places,)),
        ],
        compiler_params=pltpu.CompilerParams(vmem_limit_bytes=LIMIT),
    )(plane.reshape(1), weights)


def gather_kernel(level, plane, core, *refs):
    *sources, out, ready = refs
    copies = []
    for at, blocks in enumerate(sources):
        for step in range(blocks.shape[0]):
            place = plane[0] ^ step
            target = out.at[level[0] ^ (at % 2), place // 2, core[0] ^ (at // 2), place % 2]
            copies.append(pltpu.make_async_copy(blocks.at[step], target, ready.at[at, step]))
            copies[-1].start()
    for copy in copies:
        copy.wait()


def gather_blocks(level, plane, core, sources):
    scalar, hbm = pl.BlockSpec(memory_space=pltpu.SMEM), pl.BlockSpec(memory_space=pltpu.HBM)
    places, rows, columns = sources[0].shape
    return pl.pallas_call(
        gather_kernel,
        name="gather_blocks",
        in_specs=[scalar] * 3 + [hbm] * len(sources),
        out_specs=pl.BlockSpec(memory_space=pltpu.VMEM),
        out_shape=jax.ShapeDtypeStruct((2, places // 2, 2, 2, rows, columns), sources[0].dtype),
        scratch_shapes=[pltpu.SemaphoreType.DMA((len(sources), places))],
        compiler_params=pltpu.CompilerParams(vmem_limit_bytes=3 * 2**20),
    )(level.reshape(1), plane.reshape(1), core.reshape(1), *sources)


def dense_layer(tokens, norm_gain, expert_weights, slot_expert, pair_slots, combine_weights):
    experts, own_rows, packed = expert_weights.shape
    token_count, width = tokens.shape
    hidden_units = packed // 3
    part = hidden_units // 2
    chip_axes = ("z", "y", "x")
    chips = experts
    h, c = lax.axis_index("h"), lax.axis_index("c")
    group = lax.axis_size("x") * own_rows
    groups = width // (2 * group)

    z, plane = lax.axis_index("z"), lax.axis_index(("y", "x"))
    places = chips // 2
    keep, give = normalize(c, tokens, norm_gain, groups)
    packed, *blocks = pack(plane, expert_weights)
    gate_up = exchange(packed.reshape(2 * experts, own_rows, 2 * part), ("h",) + chip_axes)
    gate_up = gate_up.reshape(width // 2, 2 * part)

    for step in range(1, places):
        pairs = [(i, i ^ step) for i in range(places)]
        blocks[step] = lax.ppermute(blocks[step], ("y", "x"), pairs)
    kept = jnp.stack([lax.dynamic_index_in_dim(block, z, 0, keepdims=False) for block in blocks])
    passed = jnp.stack([lax.dynamic_index_in_dim(block, 1 - z, 0, keepdims=False) for block in blocks])
    kept, passed = lax.optimization_barrier((kept, passed))
    arrived = lax.ppermute(passed, "z", SWAP)
    sources = [kept, arrived, lax.ppermute(kept, "c", SWAP), lax.ppermute(arrived, "c", SWAP)]
    down = gather_blocks(z, plane, c, sources).reshape(width // 2, hidden_units)

    from_c = lax.ppermute(give, "c", SWAP)
    from_h = lax.ppermute(keep, "h", SWAP)
    from_hc = lax.ppermute(give, ("h", "c"), CROSS)
    near = jnp.stack([in_order(h, keep, from_h, 0), in_order(h, from_c, from_hc, 0)])
    column = in_order(z, near[:, None], lax.ppermute(near, "z", SWAP)[:, None], 1)
    rows = jnp.zeros((2, 2, chips // 2, 2 * token_count, width // 2), near.dtype)
    rows = lax.dynamic_update_slice(rows, column[:, :, None], (0, 0, plane, 0, 0))
    for step in range(1, chips // 2):
        pairs = [(i, i ^ step) for i in range(chips // 2)]
        arrived = lax.ppermute(column, ("y", "x"), pairs)
        rows = lax.dynamic_update_slice(rows, arrived[:, :, None], (0, 0, plane ^ step, 0, 0))
    count = chips * token_count
    rows = rows.reshape(2, 1, 2 * count, width // 2)

    other = jnp.dot(rows[1, 0], gate_up, preferred_element_type=jnp.float32).astype(jnp.bfloat16)
    arrived = lax.ppermute(other, "c", SWAP)
    kept_sums = jnp.dot(rows[0, 0], gate_up, preferred_element_type=jnp.float32)
    kept_sums, arrived = lax.optimization_barrier((kept_sums, arrived))
    pre = kept_sums + arrived.astype(jnp.float32)
    hidden = (jax.nn.silu(pre[:, :part]) * pre[:, part:]).astype(jnp.bfloat16)
    far = lax.ppermute(hidden, "h", SWAP)
    hidden, pair_slots = lax.optimization_barrier((hidden, pair_slots))
    coefficient = slot_coefficients(slot_expert, pair_slots, combine_weights, experts).T
    far_weights = lax.ppermute(coefficient, "h", SWAP)
    far, far_weights = lax.optimization_barrier((far, far_weights))
    coefficient = in_order(h, coefficient, far_weights, 1)
    hidden = in_order(h, hidden, far, 1)
    hidden = lax.optimization_barrier(hidden)
    result = lax.dot_general(hidden, down, (((1,), (1,)), ((), ())), preferred_element_type=jnp.float32)
    result = result.astype(jnp.bfloat16).reshape(chips, 2 * token_count, width // 2)
    returned = exchange(result, chip_axes).astype(jnp.float32)
    mixed = jnp.sum(returned * coefficient[:, :, None], axis=0).astype(jnp.bfloat16)
    low, high = mixed[:token_count], mixed[token_count:]
    mine, sent = jnp.where(h == 0, low, high), jnp.where(h == 0, high, low)
    return assemble(h, mine, lax.ppermute(sent, "h", SWAP))


def per_device(tokens, norm_gain, expert_weights, slot_expert, pair_slots, combine_weights):
    slot_count = lax.axis_size("dp")
    model_width = tokens.shape[1]
    packed_width = expert_weights.shape[2]
    hidden_units = packed_width // 3
    token_count = tokens.shape[0]
    choice_count = pair_slots.shape[1]
    pair_count = token_count * choice_count
    capacity = max(2, 2 * pair_count // slot_count)
    outgoing = jnp.take(expert_weights, slot_expert, axis=0)
    arrived = lax.all_to_all(outgoing, "dp", split_axis=0, concat_axis=0, tiled=True)
    assembled = lax.all_gather(arrived[:, None], "rep", axis=1, tiled=True)
    weight = assembled.reshape(model_width, packed_width)
    values = tokens.astype(jnp.float32)
    mean_square = jnp.mean(values * values, axis=1, keepdims=True)
    normed = (values * lax.rsqrt(mean_square + 1e-06) * norm_gain[None, :]).astype(jnp.bfloat16)
    targets = pair_slots.reshape(pair_count)
    onehot = (targets[:, None] == jnp.arange(slot_count, dtype=jnp.int32)[None, :]).astype(
        jnp.int32
    )
    before = jnp.cumsum(onehot, axis=0) - onehot
    position = jnp.sum(before * onehot, axis=1)
    target_row = targets * capacity + position
    selector = (
        jnp.arange(slot_count * capacity, dtype=jnp.int32)[:, None] == target_row[None, :]
    ).astype(jnp.bfloat16)
    pair_rows = jnp.repeat(normed, choice_count, axis=0)
    outbound = jnp.dot(selector, pair_rows, preferred_element_type=jnp.float32).astype(jnp.bfloat16)
    outbound = outbound.reshape(slot_count, capacity, model_width)
    rows = lax.all_to_all(outbound, "dp", split_axis=0, concat_axis=0, tiled=True).reshape(
        -1, model_width
    )
    gate_up = jnp.dot(rows, weight[:, : 2 * hidden_units], preferred_element_type=jnp.float32)
    hidden = (jax.nn.silu(gate_up[:, :hidden_units]) * gate_up[:, hidden_units:]).astype(
        jnp.bfloat16
    )
    result = lax.dot_general(
        hidden,
        weight[:, 2 * hidden_units :],
        (((1,), (1,)), ((), ())),
        preferred_element_type=jnp.float32,
    )
    result = result.astype(jnp.bfloat16).reshape(slot_count, -1, model_width)
    returned = lax.all_to_all(result, "dp", split_axis=0, concat_axis=0, tiled=True)
    expert_out = jnp.dot(
        selector.T,
        returned.reshape(slot_count * capacity, model_width),
        preferred_element_type=jnp.float32,
    )
    expert_out = expert_out.reshape(token_count, choice_count, model_width)
    mixed = jnp.sum(expert_out * combine_weights[:, :, None], axis=1)
    return mixed.astype(jnp.bfloat16)


def solution(mesh):
    slots, engines = mesh.shape["dp"], mesh.shape["rep"]

    def layer(tokens, norm_gain, expert_weights, slot_expert, pair_slots, combine_weights):
        experts = expert_weights.shape[0]
        dense = engines == 2 and slots == 2 * experts and slots % 8 == 0 and slots <= 16
        if dense:
            devices = mesh.devices.reshape(2, slots // 8, 2, 2, engines)
            inner, split = Mesh(devices, ("h", "z", "y", "c", "x")), ("h", "z", "y", "c", "x")
        else:
            inner, split = mesh, ("dp", "rep")
        placed = (P(split, None), P(), P(None, split, None), P(), P(split, None), P(split, None))
        return jax.shard_map(
            dense_layer if dense else per_device,
            mesh=inner,
            in_specs=placed,
            out_specs=P(split, None),
            check_vma=False,
        )(tokens, norm_gain, expert_weights, slot_expert, pair_slots, combine_weights)

    return layer
```

```python
import functools

import jax
import jax.numpy as jnp
from jax import lax
from jax.experimental import pallas as pl
from jax.experimental.pallas import tpu as pltpu
from jax.sharding import Mesh, PartitionSpec as P

SWAP = [(0, 1), (1, 0)]
PACK_STEPS = 2
LIMIT = 61 * 2**20
CROSS = [(0, 3), (1, 2), (2, 1), (3, 0)]


def in_order(bit, near, far, axis):
    return jnp.where(
        bit == 0, jnp.concatenate([near, far], axis=axis), jnp.concatenate([far, near], axis=axis)
    )


def slot_coefficients(slot_expert, pair_slots, combine_weights, experts, chip):
    slots = jnp.arange(slot_expert.shape[0], dtype=jnp.int32)
    held = slot_expert[None, None, :]
    chosen = jnp.sum(jnp.where(pair_slots[:, :, None] == slots[None, None, :], held, 0), axis=2)
    numbers = jnp.arange(experts, dtype=jnp.int32) ^ chip
    weights = combine_weights[:, :, None]
    return jnp.sum(jnp.where(chosen[:, :, None] == numbers[None, None, :], weights, 0.0), axis=1)


def assemble_kernel(half, mine, other, out):
    columns = mine.shape[1]
    own = pl.multiple_of(half[0] * columns, columns)
    out[:, pl.ds(own, columns)] = mine[...]
    out[:, pl.ds(columns - own, columns)] = other[...]


def assemble(half, mine, other):
    rows, columns = mine.shape
    vmem = pl.BlockSpec(memory_space=pltpu.VMEM)
    return pl.pallas_call(
        assemble_kernel,
        name="assemble",
        in_specs=[pl.BlockSpec(memory_space=pltpu.SMEM), vmem, vmem],
        out_specs=vmem,
        out_shape=jax.ShapeDtypeStruct((rows, 2 * columns), mine.dtype),
        compiler_params=pltpu.CompilerParams(vmem_limit_bytes=2**20),
    )(half.reshape(1), mine, other)


def exchange(value, axes):
    return lax.all_to_all(value, axes, 0, 0, tiled=True)


def pack_kernel(plane, weights, packed, *refs):
    places = weights.shape[0] // 2
    outs, (room, down_room, ready, done) = refs[:places], refs[places:]
    experts, _, packed_width = weights.shape
    hidden_units = packed_width // 3
    part, size = hidden_units // 2, experts // PACK_STEPS
    loads, stores, at = [], [], 0

    def load(source, target):
        nonlocal at
        loads[-1].append(pltpu.make_async_copy(source, target, ready.at[at]))
        loads[-1][-1].start()
        at += 1

    for k in range(PACK_STEPS):
        some = pl.ds(k * size, size)
        for i in range(2):
            loads.append([])
            for j in range(2):
                source = weights.at[some, :, pl.ds(j * hidden_units + i * part, part)]
                load(source, room.at[i, some, :, pl.ds(j * part, part)])
            stores.append((room.at[i, some], packed.at[i, some]))
    for step in range(places):
        loads.append([])
        for level in range(2):
            expert = level * places + (plane[0] ^ step)
            load(weights.at[expert, :, pl.ds(2 * hidden_units, hidden_units)], down_room.at[step, level])
        stores.append((down_room.at[step], outs[step]))
    writes = []
    for arriving, (source, target) in zip(loads, stores, strict=True):
        for copy in arriving:
            copy.wait()
        writes.append(pltpu.make_async_copy(source, target, done.at[len(writes)]))
        writes[-1].start()
    for copy in writes:
        copy.wait()


def normalize_kernel(groups, core, all_tokens, all_gain, keep, give, tokens, gain, first):
    loads = [
        pltpu.make_async_copy(all_tokens, tokens, first.at[0]),
        pltpu.make_async_copy(all_gain, gain, first.at[1]),
    ]
    for load in loads:
        load.start()
    for load in loads:
        load.wait()
    values = tokens[...].astype(jnp.float32)
    mean_square = jnp.mean(values * values, axis=1, keepdims=True)
    normed = (values * lax.rsqrt(mean_square + 1e-06) * gain[...]).astype(keep.dtype)
    group = normed.shape[1] // 2 // groups

    def split(first, second):
        for g in range(groups):
            at = slice(g * group, (g + 1) * group)
            first[:, at] = normed[:, 2 * g * group : (2 * g + 1) * group]
            second[:, at] = normed[:, (2 * g + 1) * group : (2 * g + 2) * group]

    @pl.when(core[0] == 0)
    def _():
        split(keep, give)

    @pl.when(core[0] != 0)
    def _():
        split(give, keep)


def normalize(core, tokens, gain, groups):
    count, width = tokens.shape
    hbm, vmem = pl.BlockSpec(memory_space=pltpu.HBM), pl.BlockSpec(memory_space=pltpu.VMEM)
    return pl.pallas_call(
        functools.partial(normalize_kernel, groups),
        name="normalize",
        in_specs=[pl.BlockSpec(memory_space=pltpu.SMEM), hbm, hbm],
        out_specs=[vmem] * 2,
        out_shape=[jax.ShapeDtypeStruct((count, width // 2), tokens.dtype)] * 2,
        scratch_shapes=[
            pltpu.VMEM((count, width), tokens.dtype),
            pltpu.VMEM((1, width), gain.dtype),
            pltpu.SemaphoreType.DMA((2,)),
        ],
        compiler_params=pltpu.CompilerParams(vmem_limit_bytes=LIMIT),
    )(core.reshape(1), tokens, gain.reshape(1, width))


def pack(plane, weights):
    experts, rows, packed_width = weights.shape
    hidden_units = packed_width // 3
    places = experts // 2
    hbm = pl.BlockSpec(memory_space=pltpu.HBM)
    block = jax.ShapeDtypeStruct((2, rows, hidden_units), weights.dtype)
    packed = jax.ShapeDtypeStruct((2, experts, rows, hidden_units), weights.dtype)
    return pl.pallas_call(
        pack_kernel,
        name="pack",
        in_specs=[pl.BlockSpec(memory_space=pltpu.SMEM), hbm],
        out_specs=[hbm] * (1 + places),
        out_shape=[packed] + [block] * places,
        scratch_shapes=[
            pltpu.VMEM(packed.shape, weights.dtype),
            pltpu.VMEM((places,) + block.shape, weights.dtype),
            pltpu.SemaphoreType.DMA((4 * PACK_STEPS + experts,)),
            pltpu.SemaphoreType.DMA((2 * PACK_STEPS + places,)),
        ],
        compiler_params=pltpu.CompilerParams(vmem_limit_bytes=LIMIT),
    )(plane.reshape(1), weights)


def gather_kernel(level, plane, core, *refs):
    *sources, out, ready = refs
    copies = []
    for at, blocks in enumerate(sources):
        for step in range(blocks.shape[0]):
            place = plane[0] ^ step
            target = out.at[level[0] ^ (at % 2), place // 2, core[0] ^ (at // 2), place % 2]
            copies.append(pltpu.make_async_copy(blocks.at[step], target, ready.at[at, step]))
            copies[-1].start()
    for copy in copies:
        copy.wait()


def gather_blocks(level, plane, core, sources):
    scalar, hbm = pl.BlockSpec(memory_space=pltpu.SMEM), pl.BlockSpec(memory_space=pltpu.HBM)
    places, rows, columns = sources[0].shape
    return pl.pallas_call(
        gather_kernel,
        name="gather_blocks",
        in_specs=[scalar] * 3 + [hbm] * len(sources),
        out_specs=pl.BlockSpec(memory_space=pltpu.VMEM),
        out_shape=jax.ShapeDtypeStruct((2, places // 2, 2, 2, rows, columns), sources[0].dtype),
        scratch_shapes=[pltpu.SemaphoreType.DMA((len(sources), places))],
        compiler_params=pltpu.CompilerParams(vmem_limit_bytes=3 * 2**20),
    )(level.reshape(1), plane.reshape(1), core.reshape(1), *sources)


def dense_layer(tokens, norm_gain, expert_weights, slot_expert, pair_slots, combine_weights):
    experts, own_rows, packed = expert_weights.shape
    token_count, width = tokens.shape
    hidden_units = packed // 3
    part = hidden_units // 2
    chip_axes = ("z", "y", "x")
    chips = experts
    h, c = lax.axis_index("h"), lax.axis_index("c")
    chip = lax.axis_index(chip_axes)
    group = lax.axis_size("x") * own_rows
    groups = width // (2 * group)

    z, plane = lax.axis_index("z"), lax.axis_index(("y", "x"))
    places = chips // 2
    keep, give = normalize(c, tokens, norm_gain, groups)
    packed, *blocks = pack(plane, expert_weights)
    gate_up = exchange(packed.reshape(2 * experts, own_rows, 2 * part), ("h",) + chip_axes)
    gate_up = gate_up.reshape(width // 2, 2 * part)

    for step in range(1, places):
        pairs = [(i, i ^ step) for i in range(places)]
        blocks[step] = lax.ppermute(blocks[step], ("y", "x"), pairs)
    kept = jnp.stack([lax.dynamic_index_in_dim(block, z, 0, keepdims=False) for block in blocks])
    passed = jnp.stack([lax.dynamic_index_in_dim(block, 1 - z, 0, keepdims=False) for block in blocks])
    kept, passed = lax.optimization_barrier((kept, passed))
    arrived = lax.ppermute(passed, "z", SWAP)
    sources = [kept, arrived, lax.ppermute(kept, "c", SWAP), lax.ppermute(arrived, "c", SWAP)]
    down = gather_blocks(z, plane, c, sources).reshape(width // 2, hidden_units)

    from_c = lax.ppermute(give, "c", SWAP)
    from_h = lax.ppermute(keep, "h", SWAP)
    from_hc = lax.ppermute(give, ("h", "c"), CROSS)
    near = jnp.stack([in_order(h, keep, from_h, 0), in_order(h, from_c, from_hc, 0)])
    column = jnp.stack([near, lax.ppermute(near, "z", SWAP)], axis=1)
    rows = [column]
    for step in range(1, places):
        pairs = [(i, i ^ step) for i in range(places)]
        rows.append(lax.ppermute(column, ("y", "x"), pairs))
    rows = jnp.stack(rows, axis=2)
    count = chips * token_count
    rows = rows.reshape(2, 1, 2 * count, width // 2)

    other = jnp.dot(rows[1, 0], gate_up, preferred_element_type=jnp.float32).astype(jnp.bfloat16)
    arrived = lax.ppermute(other, "c", SWAP)
    kept_sums = jnp.dot(rows[0, 0], gate_up, preferred_element_type=jnp.float32)
    kept_sums, arrived = lax.optimization_barrier((kept_sums, arrived))
    pre = kept_sums + arrived.astype(jnp.float32)
    hidden = (jax.nn.silu(pre[:, :part]) * pre[:, part:]).astype(jnp.bfloat16)
    far = lax.ppermute(hidden, "h", SWAP)
    hidden, pair_slots = lax.optimization_barrier((hidden, pair_slots))
    coefficient = slot_coefficients(slot_expert, pair_slots, combine_weights, experts, chip).T
    far_weights = lax.ppermute(coefficient, "h", SWAP)
    far, far_weights = lax.optimization_barrier((far, far_weights))
    coefficient = in_order(h, coefficient, far_weights, 1)
    hidden = in_order(h, hidden, far, 1)
    hidden = lax.optimization_barrier(hidden)
    result = lax.dot_general(hidden, down, (((1,), (1,)), ((), ())), preferred_element_type=jnp.float32)
    result = result.astype(jnp.bfloat16).reshape(chips, 2 * token_count, width // 2)
    returned = [result[0]]
    for step in range(1, chips):
        pairs = [(i, i ^ step) for i in range(chips)]
        returned.append(lax.ppermute(result[step], chip_axes, pairs))
    terms = [block.astype(jnp.float32) * coefficient[at][:, None] for at, block in enumerate(returned)]
    mixed = sum(terms).astype(jnp.bfloat16)
    low, high = mixed[:token_count], mixed[token_count:]
    mine, sent = jnp.where(h == 0, low, high), jnp.where(h == 0, high, low)
    return assemble(h, mine, lax.ppermute(sent, "h", SWAP))


def per_device(tokens, norm_gain, expert_weights, slot_expert, pair_slots, combine_weights):
    slot_count = lax.axis_size("dp")
    model_width = tokens.shape[1]
    packed_width = expert_weights.shape[2]
    hidden_units = packed_width // 3
    token_count = tokens.shape[0]
    choice_count = pair_slots.shape[1]
    pair_count = token_count * choice_count
    capacity = max(2, 2 * pair_count // slot_count)
    outgoing = jnp.take(expert_weights, slot_expert, axis=0)
    arrived = lax.all_to_all(outgoing, "dp", split_axis=0, concat_axis=0, tiled=True)
    assembled = lax.all_gather(arrived[:, None], "rep", axis=1, tiled=True)
    weight = assembled.reshape(model_width, packed_width)
    values = tokens.astype(jnp.float32)
    mean_square = jnp.mean(values * values, axis=1, keepdims=True)
    normed = (values * lax.rsqrt(mean_square + 1e-06) * norm_gain[None, :]).astype(jnp.bfloat16)
    targets = pair_slots.reshape(pair_count)
    onehot = (targets[:, None] == jnp.arange(slot_count, dtype=jnp.int32)[None, :]).astype(
        jnp.int32
    )
    before = jnp.cumsum(onehot, axis=0) - onehot
    position = jnp.sum(before * onehot, axis=1)
    target_row = targets * capacity + position
    selector = (
        jnp.arange(slot_count * capacity, dtype=jnp.int32)[:, None] == target_row[None, :]
    ).astype(jnp.bfloat16)
    pair_rows = jnp.repeat(normed, choice_count, axis=0)
    outbound = jnp.dot(selector, pair_rows, preferred_element_type=jnp.float32).astype(jnp.bfloat16)
    outbound = outbound.reshape(slot_count, capacity, model_width)
    rows = lax.all_to_all(outbound, "dp", split_axis=0, concat_axis=0, tiled=True).reshape(
        -1, model_width
    )
    gate_up = jnp.dot(rows, weight[:, : 2 * hidden_units], preferred_element_type=jnp.float32)
    hidden = (jax.nn.silu(gate_up[:, :hidden_units]) * gate_up[:, hidden_units:]).astype(
        jnp.bfloat16
    )
    result = lax.dot_general(
        hidden,
        weight[:, 2 * hidden_units :],
        (((1,), (1,)), ((), ())),
        preferred_element_type=jnp.float32,
    )
    result = result.astype(jnp.bfloat16).reshape(slot_count, -1, model_width)
    returned = lax.all_to_all(result, "dp", split_axis=0, concat_axis=0, tiled=True)
    expert_out = jnp.dot(
        selector.T,
        returned.reshape(slot_count * capacity, model_width),
        preferred_element_type=jnp.float32,
    )
    expert_out = expert_out.reshape(token_count, choice_count, model_width)
    mixed = jnp.sum(expert_out * combine_weights[:, :, None], axis=1)
    return mixed.astype(jnp.bfloat16)


def solution(mesh):
    slots, engines = mesh.shape["dp"], mesh.shape["rep"]

    def layer(tokens, norm_gain, expert_weights, slot_expert, pair_slots, combine_weights):
        experts = expert_weights.shape[0]
        dense = engines == 2 and slots == 2 * experts and slots % 8 == 0 and slots <= 16
        if dense:
            devices = mesh.devices.reshape(2, slots // 8, 2, 2, engines)
            inner, split = Mesh(devices, ("h", "z", "y", "c", "x")), ("h", "z", "y", "c", "x")
        else:
            inner, split = mesh, ("dp", "rep")
        placed = (P(split, None), P(), P(None, split, None), P(), P(split, None), P(split, None))
        return jax.shard_map(
            dense_layer if dense else per_device,
            mesh=inner,
            in_specs=placed,
            out_specs=P(split, None),
            check_vma=False,
        )(tokens, norm_gain, expert_weights, slot_expert, pair_slots, combine_weights)

    return layer
```

```python
import functools

import jax
import jax.numpy as jnp
from jax import lax
from jax.experimental import pallas as pl
from jax.experimental.pallas import tpu as pltpu
from jax.sharding import Mesh, PartitionSpec as P

SWAP = [(0, 1), (1, 0)]
PACK_STEPS = 2
LIMIT = 61 * 2**20
CROSS = [(0, 3), (1, 2), (2, 1), (3, 0)]


def in_order(bit, near, far, axis):
    return jnp.where(
        bit == 0, jnp.concatenate([near, far], axis=axis), jnp.concatenate([far, near], axis=axis)
    )


def slot_coefficients(slot_expert, pair_slots, combine_weights, experts, chip):
    slots = jnp.arange(slot_expert.shape[0], dtype=jnp.int32)
    held = slot_expert[None, None, :]
    chosen = jnp.sum(jnp.where(pair_slots[:, :, None] == slots[None, None, :], held, 0), axis=2)
    numbers = jnp.arange(experts, dtype=jnp.int32) ^ chip
    weights = combine_weights[:, :, None]
    return jnp.sum(jnp.where(chosen[:, :, None] == numbers[None, None, :], weights, 0.0), axis=1)


def exchange(value, axes):
    return lax.all_to_all(value, axes, 0, 0, tiled=True)


def pack_kernel(plane, weights, packed, *refs):
    places = weights.shape[0] // 2
    outs, (room, down_room, ready, done) = refs[:places], refs[places:]
    experts, _, packed_width = weights.shape
    hidden_units = packed_width // 3
    part, size = hidden_units // 2, experts // PACK_STEPS
    loads, stores, at = [], [], 0

    def load(source, target):
        nonlocal at
        loads[-1].append(pltpu.make_async_copy(source, target, ready.at[at]))
        loads[-1][-1].start()
        at += 1

    for k in range(PACK_STEPS):
        some = pl.ds(k * size, size)
        for i in range(2):
            loads.append([])
            for j in range(2):
                source = weights.at[some, :, pl.ds(j * hidden_units + i * part, part)]
                load(source, room.at[i, some, :, pl.ds(j * part, part)])
            stores.append((room.at[i, some], packed.at[i, some]))
    for step in range(places):
        loads.append([])
        for level in range(2):
            expert = level * places + (plane[0] ^ step)
            load(weights.at[expert, :, pl.ds(2 * hidden_units, hidden_units)], down_room.at[step, level])
        stores.append((down_room.at[step], outs[step]))
    writes = []
    for arriving, (source, target) in zip(loads, stores, strict=True):
        for copy in arriving:
            copy.wait()
        writes.append(pltpu.make_async_copy(source, target, done.at[len(writes)]))
        writes[-1].start()
    for copy in writes:
        copy.wait()


def normalize_kernel(groups, core, all_tokens, all_gain, keep, give, tokens, gain, first):
    loads = [
        pltpu.make_async_copy(all_tokens, tokens, first.at[0]),
        pltpu.make_async_copy(all_gain, gain, first.at[1]),
    ]
    for load in loads:
        load.start()
    for load in loads:
        load.wait()
    values = tokens[...].astype(jnp.float32)
    mean_square = jnp.mean(values * values, axis=1, keepdims=True)
    normed = (values * lax.rsqrt(mean_square + 1e-06) * gain[...]).astype(keep.dtype)
    group = normed.shape[1] // 2 // groups

    def split(first, second):
        for g in range(groups):
            at = slice(g * group, (g + 1) * group)
            first[:, at] = normed[:, 2 * g * group : (2 * g + 1) * group]
            second[:, at] = normed[:, (2 * g + 1) * group : (2 * g + 2) * group]

    @pl.when(core[0] == 0)
    def _():
        split(keep, give)

    @pl.when(core[0] != 0)
    def _():
        split(give, keep)


def normalize(core, tokens, gain, groups):
    count, width = tokens.shape
    hbm, vmem = pl.BlockSpec(memory_space=pltpu.HBM), pl.BlockSpec(memory_space=pltpu.VMEM)
    return pl.pallas_call(
        functools.partial(normalize_kernel, groups),
        name="normalize",
        in_specs=[pl.BlockSpec(memory_space=pltpu.SMEM), hbm, hbm],
        out_specs=[vmem] * 2,
        out_shape=[jax.ShapeDtypeStruct((count, width // 2), tokens.dtype)] * 2,
        scratch_shapes=[
            pltpu.VMEM((count, width), tokens.dtype),
            pltpu.VMEM((1, width), gain.dtype),
            pltpu.SemaphoreType.DMA((2,)),
        ],
        compiler_params=pltpu.CompilerParams(vmem_limit_bytes=LIMIT),
    )(core.reshape(1), tokens, gain.reshape(1, width))


def pack(plane, weights):
    experts, rows, packed_width = weights.shape
    hidden_units = packed_width // 3
    places = experts // 2
    hbm = pl.BlockSpec(memory_space=pltpu.HBM)
    block = jax.ShapeDtypeStruct((2, rows, hidden_units), weights.dtype)
    packed = jax.ShapeDtypeStruct((2, experts, rows, hidden_units), weights.dtype)
    return pl.pallas_call(
        pack_kernel,
        name="pack",
        in_specs=[pl.BlockSpec(memory_space=pltpu.SMEM), hbm],
        out_specs=[hbm] * (1 + places),
        out_shape=[packed] + [block] * places,
        scratch_shapes=[
            pltpu.VMEM(packed.shape, weights.dtype),
            pltpu.VMEM((places,) + block.shape, weights.dtype),
            pltpu.SemaphoreType.DMA((4 * PACK_STEPS + experts,)),
            pltpu.SemaphoreType.DMA((2 * PACK_STEPS + places,)),
        ],
        compiler_params=pltpu.CompilerParams(vmem_limit_bytes=LIMIT),
    )(plane.reshape(1), weights)


def gather_kernel(level, plane, core, *refs):
    *sources, out, ready = refs
    copies = []
    for at, blocks in enumerate(sources):
        for step in range(blocks.shape[0]):
            place = plane[0] ^ step
            target = out.at[level[0] ^ (at % 2), place // 2, core[0] ^ (at // 2), place % 2]
            copies.append(pltpu.make_async_copy(blocks.at[step], target, ready.at[at, step]))
            copies[-1].start()
    for copy in copies:
        copy.wait()


def gather_blocks(level, plane, core, sources):
    scalar, hbm = pl.BlockSpec(memory_space=pltpu.SMEM), pl.BlockSpec(memory_space=pltpu.HBM)
    places, rows, columns = sources[0].shape
    return pl.pallas_call(
        gather_kernel,
        name="gather_blocks",
        in_specs=[scalar] * 3 + [hbm] * len(sources),
        out_specs=pl.BlockSpec(memory_space=pltpu.VMEM),
        out_shape=jax.ShapeDtypeStruct((2, places // 2, 2, 2, rows, columns), sources[0].dtype),
        scratch_shapes=[pltpu.SemaphoreType.DMA((len(sources), places))],
        compiler_params=pltpu.CompilerParams(vmem_limit_bytes=3 * 2**20),
    )(level.reshape(1), plane.reshape(1), core.reshape(1), *sources)


def dense_layer(tokens, norm_gain, expert_weights, slot_expert, pair_slots, combine_weights):
    experts, own_rows, packed = expert_weights.shape
    token_count, width = tokens.shape
    hidden_units = packed // 3
    part = hidden_units // 2
    chip_axes = ("z", "y", "x")
    chips = experts
    h, c = lax.axis_index("h"), lax.axis_index("c")
    chip = lax.axis_index(chip_axes)
    group = lax.axis_size("x") * own_rows
    groups = width // (2 * group)

    z, plane = lax.axis_index("z"), lax.axis_index(("y", "x"))
    places = chips // 2
    keep, give = normalize(c, tokens, norm_gain, groups)
    packed, *blocks = pack(plane, expert_weights)
    gate_up = exchange(packed.reshape(2 * experts, own_rows, 2 * part), ("h",) + chip_axes)
    gate_up = gate_up.reshape(width // 2, 2 * part)

    for step in range(1, places):
        pairs = [(i, i ^ step) for i in range(places)]
        blocks[step] = lax.ppermute(blocks[step], ("y", "x"), pairs)
    kept = jnp.stack([lax.dynamic_index_in_dim(block, z, 0, keepdims=False) for block in blocks])
    passed = jnp.stack([lax.dynamic_index_in_dim(block, 1 - z, 0, keepdims=False) for block in blocks])
    kept, passed = lax.optimization_barrier((kept, passed))
    arrived = lax.ppermute(passed, "z", SWAP)
    sources = [kept, arrived, lax.ppermute(kept, "c", SWAP), lax.ppermute(arrived, "c", SWAP)]
    down = gather_blocks(z, plane, c, sources).reshape(width // 2, hidden_units)

    from_c = lax.ppermute(give, "c", SWAP)
    from_h = lax.ppermute(keep, "h", SWAP)
    from_hc = lax.ppermute(give, ("h", "c"), CROSS)
    near = jnp.stack([in_order(h, keep, from_h, 0), in_order(h, from_c, from_hc, 0)])
    column = jnp.stack([near, lax.ppermute(near, "z", SWAP)], axis=1)
    rows = [column]
    for step in range(1, places):
        pairs = [(i, i ^ step) for i in range(places)]
        rows.append(lax.ppermute(column, ("y", "x"), pairs))
    rows = jnp.stack(rows, axis=2)
    count = chips * token_count
    rows = rows.reshape(2, 1, 2 * count, width // 2)

    other = jnp.dot(rows[1, 0], gate_up, preferred_element_type=jnp.float32).astype(jnp.bfloat16)
    arrived = lax.ppermute(other, "c", SWAP)
    kept_sums = jnp.dot(rows[0, 0], gate_up, preferred_element_type=jnp.float32)
    kept_sums, arrived = lax.optimization_barrier((kept_sums, arrived))
    pre = kept_sums + arrived.astype(jnp.float32)
    hidden = (jax.nn.silu(pre[:, :part]) * pre[:, part:]).astype(jnp.bfloat16)
    far = lax.ppermute(hidden, "h", SWAP)
    hidden, pair_slots = lax.optimization_barrier((hidden, pair_slots))
    coefficient = slot_coefficients(slot_expert, pair_slots, combine_weights, experts, chip).T
    far_weights = lax.ppermute(coefficient, "h", SWAP)
    far, far_weights = lax.optimization_barrier((far, far_weights))
    coefficient = in_order(h, coefficient, far_weights, 1)
    hidden = in_order(h, hidden, far, 1)
    hidden = lax.optimization_barrier(hidden)
    result = lax.dot_general(hidden, down, (((1,), (1,)), ((), ())), preferred_element_type=jnp.float32)
    result = result.astype(jnp.bfloat16).reshape(chips, 2 * token_count, width // 2)
    returned = [result[0]]
    for step in range(1, chips):
        pairs = [(i, i ^ step) for i in range(chips)]
        returned.append(lax.ppermute(result[step], chip_axes, pairs))
    terms = [block.astype(jnp.float32) * coefficient[at][:, None] for at, block in enumerate(returned)]
    mixed = sum(terms).astype(jnp.bfloat16)
    low, high = mixed[:token_count], mixed[token_count:]
    mine, sent = jnp.where(h == 0, low, high), jnp.where(h == 0, high, low)
    return in_order(h, mine, lax.ppermute(sent, "h", SWAP), 1)


def per_device(tokens, norm_gain, expert_weights, slot_expert, pair_slots, combine_weights):
    slot_count = lax.axis_size("dp")
    model_width = tokens.shape[1]
    packed_width = expert_weights.shape[2]
    hidden_units = packed_width // 3
    token_count = tokens.shape[0]
    choice_count = pair_slots.shape[1]
    pair_count = token_count * choice_count
    capacity = max(2, 2 * pair_count // slot_count)
    outgoing = jnp.take(expert_weights, slot_expert, axis=0)
    arrived = lax.all_to_all(outgoing, "dp", split_axis=0, concat_axis=0, tiled=True)
    assembled = lax.all_gather(arrived[:, None], "rep", axis=1, tiled=True)
    weight = assembled.reshape(model_width, packed_width)
    values = tokens.astype(jnp.float32)
    mean_square = jnp.mean(values * values, axis=1, keepdims=True)
    normed = (values * lax.rsqrt(mean_square + 1e-06) * norm_gain[None, :]).astype(jnp.bfloat16)
    targets = pair_slots.reshape(pair_count)
    onehot = (targets[:, None] == jnp.arange(slot_count, dtype=jnp.int32)[None, :]).astype(
        jnp.int32
    )
    before = jnp.cumsum(onehot, axis=0) - onehot
    position = jnp.sum(before * onehot, axis=1)
    target_row = targets * capacity + position
    selector = (
        jnp.arange(slot_count * capacity, dtype=jnp.int32)[:, None] == target_row[None, :]
    ).astype(jnp.bfloat16)
    pair_rows = jnp.repeat(normed, choice_count, axis=0)
    outbound = jnp.dot(selector, pair_rows, preferred_element_type=jnp.float32).astype(jnp.bfloat16)
    outbound = outbound.reshape(slot_count, capacity, model_width)
    rows = lax.all_to_all(outbound, "dp", split_axis=0, concat_axis=0, tiled=True).reshape(
        -1, model_width
    )
    gate_up = jnp.dot(rows, weight[:, : 2 * hidden_units], preferred_element_type=jnp.float32)
    hidden = (jax.nn.silu(gate_up[:, :hidden_units]) * gate_up[:, hidden_units:]).astype(
        jnp.bfloat16
    )
    result = lax.dot_general(
        hidden,
        weight[:, 2 * hidden_units :],
        (((1,), (1,)), ((), ())),
        preferred_element_type=jnp.float32,
    )
    result = result.astype(jnp.bfloat16).reshape(slot_count, -1, model_width)
    returned = lax.all_to_all(result, "dp", split_axis=0, concat_axis=0, tiled=True)
    expert_out = jnp.dot(
        selector.T,
        returned.reshape(slot_count * capacity, model_width),
        preferred_element_type=jnp.float32,
    )
    expert_out = expert_out.reshape(token_count, choice_count, model_width)
    mixed = jnp.sum(expert_out * combine_weights[:, :, None], axis=1)
    return mixed.astype(jnp.bfloat16)


def solution(mesh):
    slots, engines = mesh.shape["dp"], mesh.shape["rep"]

    def layer(tokens, norm_gain, expert_weights, slot_expert, pair_slots, combine_weights):
        experts = expert_weights.shape[0]
        dense = engines == 2 and slots == 2 * experts and slots % 8 == 0 and slots <= 16
        if dense:
            devices = mesh.devices.reshape(2, slots // 8, 2, 2, engines)
            inner, split = Mesh(devices, ("h", "z", "y", "c", "x")), ("h", "z", "y", "c", "x")
        else:
            inner, split = mesh, ("dp", "rep")
        placed = (P(split, None), P(), P(None, split, None), P(), P(split, None), P(split, None))
        return jax.shard_map(
            dense_layer if dense else per_device,
            mesh=inner,
            in_specs=placed,
            out_specs=P(split, None),
            check_vma=False,
        )(tokens, norm_gain, expert_weights, slot_expert, pair_slots, combine_weights)

    return layer
```
